256 devices in a mesh: seq: 64 (over y, z, core), head: 4 (over x).
Axes of the slice: x: 4, y: 4, z: 8, core: 2. Of those that a mesh axis runs over, the one named last changes fastest.
Arguments:
- queries: float32 [8192, 4096], P('seq', 'head'), may hold values from -6 to 6
- key_rows: float32 [8192, 4096], P('seq', 'head'), may hold values from -6 to 6
- value_rows: float32 [8192, 4096], P('seq', 'head'), may hold values from -6 to 6
- target: float32 [8192, 4096], P('seq', 'head'), may hold values from -6 to 6
- norm_gain: float32 [4096], P('head'), may hold values from 0.1 to 1.9
- valid_mask: int32 [8192], P('seq'), may hold values from 0 to 1, as said below
Outputs:
- grad_queries: float32 [8192, 4096], P('seq', 'head')
- grad_keys: float32 [8192, 4096], P('seq', 'head')
- grad_values: float32 [8192, 4096], P('seq', 'head')
- loss_value: float32 [], replicated
The draws below stay inside these ranges and needn't reach their ends.
Inputs may be any that keep to these rules, and one draw needn't show every extreme that they name: `valid_mask`: the last token of the sequence is valid.
All inputs are finite; a program needn't handle non-finite values.
Results may differ from the reference program's by a relative error of at most 0.0003.
Values sent between devices are 32-bit elements; how exact they have to be, the bound alone decides.
A program may use at most 64 MiB of HBM per device.

```python
import jax
import jax.numpy as jnp
from jax import lax

HEADS = 32
HEAD_DIM = 128
TOK_DEV = 128
TOKENS = 8192
WIDTH = 4096


def draw_value_rows(key, part):
    array_shape = (TOKENS, HEADS * HEAD_DIM)
    return jnp.clip(jax.random.normal(key, array_shape, jnp.float32), -6.0, 6.0)


def draw_valid_mask(key, part):
    position = jnp.arange(TOKENS, dtype=jnp.int32)
    ticket = jax.random.randint(key, (TOKENS,), 0, 4 * TOKENS, dtype=jnp.int32)
    chosen = (ticket < TOKENS + 2 * position).astype(jnp.int32)
    return jnp.where(position == TOKENS - 1, 1, chosen).astype(jnp.int32)


def levels(key, shape, cuts, low, top_value):
    factor_of, own = 1.0, jax.random.fold_in(key, 6)
    for axis_at, shards_of in cuts:
        draws = jnp.exp(jax.random.uniform(jax.random.fold_in(own, axis_at), (shards_of,), jnp.float32, low / len(cuts), top_value / len(cuts)))
        factor_of = factor_of * jnp.repeat(draws, shape[axis_at] // shards_of).reshape([-1 if axis == axis_at else 1 for axis in range(len(shape))])
    return factor_of


def gaussian(stream_key, shape, width, limit, shards=(), held_as=jnp.bfloat16):
    factor_of = levels(stream_key, shape, shards, -0.22, 0.18) if shards else 1.0
    drawn = jax.random.normal(stream_key, shape, jnp.float32) * width * factor_of
    return jnp.minimum(jnp.maximum(drawn, -limit), limit).astype(held_as)


def setup_inputs(seed: int = 0) -> dict:
    splits = jax.random.split(jax.random.key(seed), 7)
    return {
        "queries": gaussian(splits[0], (TOKENS, WIDTH), 1.0, 6.0, ((0, 64), (1, 4)), jnp.float32),
        "key_rows": gaussian(splits[1], (TOKENS, WIDTH), 1.0, 6.0, ((0, 64), (1, 4)), jnp.float32),
        "value_rows": draw_value_rows(jax.random.fold_in(splits[6], 71), 0),
        "target": gaussian(splits[3], (TOKENS, WIDTH), 1.0, 6.0, ((0, 64), (1, 4)), jnp.float32),
        "norm_gain": jnp.clip(1.0 + 0.18 * jax.random.normal(splits[4], (WIDTH,), jnp.float32), 0.1, 1.9),
        "valid_mask": draw_valid_mask(jax.random.fold_in(splits[6], 71), 0),
    }


epsilon = 1e-06

def reference(queries, key_rows, value_rows, target, norm_gain, valid_mask):
    highest = lax.Precision.HIGHEST
    blocks = TOKENS // TOK_DEV

    def to_blocks(array):
        return array.reshape(blocks, TOK_DEV, HEADS, HEAD_DIM)
    causal = jnp.tril(jnp.ones((TOK_DEV, TOK_DEV), jnp.float32))
    empty_state = jnp.zeros((HEADS, HEAD_DIM, HEAD_DIM), jnp.float32)

    def forward_block(carried, inputs):
        query_heads, key_heads, value_heads = inputs
        scores = jnp.einsum('the,she->hts', query_heads, key_heads, precision=highest) * causal
        output = jnp.einsum('hts,shf->thf', scores, value_heads, precision=highest)
        output = output + jnp.einsum('the,hef->thf', query_heads, carried, precision=highest)
        updated = carried + jnp.einsum('the,thf->hef', key_heads, value_heads, precision=highest)
        return (updated, (output, carried))
    query_blocks = to_blocks(queries)
    key_blocks = to_blocks(key_rows)
    value_blocks = to_blocks(value_rows)
    unused, (outputs, prior_states) = lax.scan(forward_block, empty_state, (query_blocks, key_blocks, value_blocks))
    attended = outputs.reshape(TOKENS, WIDTH)
    mask_float = valid_mask.astype(jnp.float32)
    weighted = mask_float[:, None] * target
    token_total = jnp.sum(mask_float)
    inverse_rms = lax.rsqrt(lax.optimization_barrier(jnp.mean(attended * attended, axis=1)) + epsilon)
    normed = attended * inverse_rms[:, None] * norm_gain
    loss_value = jnp.sum(weighted * normed) / token_total
    gain_dots = lax.optimization_barrier(jnp.sum(norm_gain * weighted * attended, axis=1))
    scale_factor = TOKENS / token_total
    grad_out = scale_factor * inverse_rms[:, None] * (norm_gain * weighted - attended * (inverse_rms * inverse_rms * gain_dots / WIDTH)[:, None])

    def backward_block(carried, inputs):
        query_heads, key_heads, value_heads, grad_heads, prior_state = inputs
        grad_scores = jnp.einsum('thf,shf->hts', grad_heads, value_heads, precision=highest) * causal
        scores = jnp.einsum('the,she->hts', query_heads, key_heads, precision=highest) * causal
        grad_query = jnp.einsum('hts,she->the', grad_scores, key_heads, precision=highest)
        grad_query = grad_query + jnp.einsum('thf,hef->the', grad_heads, prior_state, precision=highest)
        grad_key = jnp.einsum('hts,the->she', grad_scores, query_heads, precision=highest)
        grad_key = grad_key + jnp.einsum('shf,hef->she', value_heads, carried, precision=highest)
        grad_value = jnp.einsum('hts,thf->shf', scores, grad_heads, precision=highest)
        grad_value = grad_value + jnp.einsum('she,hef->shf', key_heads, carried, precision=highest)
        updated = carried + jnp.einsum('the,thf->hef', query_heads, grad_heads, precision=highest)
        return (updated, (grad_query, grad_key, grad_value))
    unused_back, (grad_q_blocks, grad_k_blocks, grad_v_blocks) = lax.scan(backward_block, empty_state, (query_blocks, key_blocks, value_blocks, to_blocks(grad_out), prior_states), reverse=True)
    return (grad_q_blocks.reshape(TOKENS, WIDTH), grad_k_blocks.reshape(TOKENS, WIDTH), grad_v_blocks.reshape(TOKENS, WIDTH), loss_value)
```

```python
import jax
import jax.numpy as jnp
from jax import lax
from jax.experimental import pallas as pl
from jax.experimental.pallas import tpu as pltpu
from jax.sharding import PartitionSpec as P

HEAD_DIM = 128
WIDTH = 4096
TOKENS = 8192
HEADS = 8
OWN = 4
CHUNKS = 2
BOTH = OWN // CHUNKS
YS, ZS, XS = 4, 8, 4
CHIPS = YS * ZS
CHUNK_ROWS = BOTH * HEAD_DIM
ROWS = CHUNK_ROWS // CHIPS
EPSILON = 1e-06

F32 = jnp.float32
BF16 = jnp.bfloat16
MESH = pl.DeviceIdType.MESH
PAIR, OUT, BACK = 0, 2, 4
FORWARD, REVERSE = 0, 6
INPUTS, SUMS, STAT_Z, STAT_Y, RESULTS, COUNT = 12, 17, 18, 19, 20, 23


def ring(delta, count):
    return min(delta, count - delta)


OFFSETS = sorted(
    ((dy, dz) for dy in range(YS) for dz in range(ZS) if dy or dz),
    key=lambda o: -(ring(o[0], YS) + ring(o[1], ZS)),
)


def split(x):
    high = x.astype(BF16)
    return high, (x - high.astype(F32)).astype(BF16)


def dot3(a, b, contract):
    dims = ((contract[:1], contract[1:]), ((), ()))

    def one(x, y):
        return lax.dot_general(x, y, dims, preferred_element_type=F32)

    return one(a[0], b[0]) + (one(a[0], b[1]) + one(a[1], b[0]))


NN, NT, TN = (1, 0), (1, 1), (0, 0)


def kernel(
    q_hbm, k_hbm, v_hbm, t_hbm, gain_ref, mask_ref,
    gq_hbm, gk_hbm, gv_hbm, loss_ref,
    k_all, v_all, q, k, v, t, mask,
    qh, ql, kh, kl, vh, vl, sh, sl, att, g, gq, gk, gv, acc,
    kv, kv_far, other, comb, recv, pre, part,
    qg, qg_one, comb_b, recv_b, pre_b, part_b,
    row_out, row_in, stat_z_out, stat_z, stat_y_out, stat_y,
    load_sems, store_sem, send_sems, recv_sems,
):
    s, x = lax.axis_index("seq"), lax.axis_index("head")
    y, z, c = s // 16, (s // 2) % ZS, s % 2
    me = y * ZS + z
    far = 1 - c

    def at(ty, tz, tc, tx):
        return (ty * 16 + tz * 2 + tc, tx)

    partner = at(y, z, far, x)
    chips = [((y + dy) % YS, (z + dz) % ZS) for dy, dz in OFFSETS]
    across = [at(y, z, tc, (x + d) % XS) for d in (2, 1, 3) for tc in range(2)] + [partner]
    greeted = [at(ty, tz, c, x) for ty, tz in chips] + across
    barrier = pltpu.get_barrier_semaphore()
    for device in greeted:
        pl.semaphore_signal(barrier, inc=1, device_id=device, device_id_type=MESH)

    def heads_of(core):
        return pl.ds(pl.multiple_of(core * OWN * HEAD_DIM, HEAD_DIM), OWN * HEAD_DIM)

    def head(i):
        return pl.ds(pl.multiple_of(i * HEAD_DIM, HEAD_DIM), HEAD_DIM)

    loads = [
        pltpu.make_async_copy(k_hbm, k_all, load_sems.at[0]),
        pltpu.make_async_copy(v_hbm, v_all, load_sems.at[1]),
        pltpu.make_async_copy(q_hbm.at[:, heads_of(c)], q.at[c], load_sems.at[2]),
        pltpu.make_async_copy(t_hbm.at[:, heads_of(c)], t.at[c], load_sems.at[3]),
    ]
    for copy in loads:
        copy.start()

    def send(src, dst, sem, device):
        pltpu.make_async_remote_copy(
            src_ref=src, dst_ref=dst, send_sem=send_sems.at[sem], recv_sem=recv_sems.at[sem],
            device_id=device, device_id_type=MESH,
        ).start()

    def arrived(ref, sem):
        pltpu.make_async_copy(ref, ref, recv_sems.at[sem]).wait()

    def sent(ref, sem):
        pltpu.make_async_copy(ref, ref, send_sems.at[sem]).wait()

    def piece(chunk, i):
        return pl.ds(pl.multiple_of(chunk * CHUNK_ROWS + i * ROWS, ROWS), ROWS)

    all_but_one = pl.ds(0, (CHIPS - 1) * ROWS)

    def rows_of(i):
        return pl.ds(pl.multiple_of(i * HEAD_DIM, HEAD_DIM), HEAD_DIM)

    def spread(comb, recv, base, chunk):
        for ty, tz in chips:
            send(comb.at[piece(chunk, ty * ZS + tz)], recv.at[piece(chunk, me)], base + OUT + chunk, at(ty, tz, c, x))
        recv[piece(chunk, me), :] = comb[piece(chunk, me), :]

    def scan(recv, pre, part, base, chunk, reverse):
        arrived(recv.at[all_but_one], base + OUT + chunk)
        total = jnp.zeros((ROWS, HEAD_DIM), F32)
        for i in reversed(range(CHIPS)) if reverse else range(CHIPS):
            pre[piece(chunk, i), :] = total
            total = total + recv[piece(chunk, i), :]
        for ty, tz in chips:
            send(pre.at[piece(chunk, ty * ZS + tz)], part.at[piece(chunk, me)], base + BACK + chunk, at(ty, tz, c, x))
        part[piece(chunk, me), :] = pre[piece(chunk, me), :]

    def scanned(part, base, chunk):
        arrived(part.at[all_but_one], base + BACK + chunk)

    loads[0].wait()
    loads[1].wait()

    def outer_far(i, carry):
        columns = head(far * OWN + i)
        kv_far[i] = dot3(split(k_all[:, columns]), split(v_all[:, columns]), TN)
        return carry

    def outer_own(i, carry):
        columns = head(c * OWN + i)
        key, value = split(k_all[:, columns]), split(v_all[:, columns])
        kh[c, i], kl[c, i] = key
        vh[c, i], vl[c, i] = value
        kv[i] = dot3(key, value, TN)
        return carry

    lax.fori_loop(0, OWN, outer_far, 0, unroll=2)
    lax.fori_loop(0, OWN, outer_own, 0, unroll=2)
    pl.semaphore_wait(barrier, len(greeted))
    for chunk in range(CHUNKS):
        half = pl.ds(chunk * BOTH, BOTH)
        send(kv_far.at[half], other.at[half], FORWARD + PAIR + chunk, partner)
    for chunk in range(CHUNKS):
        arrived(other.at[pl.ds(0, BOTH)], FORWARD + PAIR + chunk)
        for i in range(chunk * BOTH, (chunk + 1) * BOTH):
            comb[rows_of(i), :] = kv[i] + other[i]
        spread(comb, recv, FORWARD, chunk)

    send(q_hbm.at[:, heads_of(far)], q.at[c], INPUTS, partner)
    send(k_hbm.at[:, heads_of(far)], k, INPUTS + 1, partner)
    send(v_hbm.at[:, heads_of(far)], v, INPUTS + 2, partner)
    send(t_hbm.at[:, heads_of(far)], t.at[c], INPUTS + 3, partner)
    mask[c] = jnp.broadcast_to(mask_ref[...].astype(F32), (8, HEAD_DIM))
    send(mask.at[c], mask.at[c], INPUTS + 4, partner)

    token = lax.broadcasted_iota(jnp.int32, (HEAD_DIM, HEAD_DIM), 0)
    column = lax.broadcasted_iota(jnp.int32, (HEAD_DIM, HEAD_DIM), 1)
    causal = token >= column

    def as_columns(row):
        return jnp.transpose(jnp.broadcast_to(row, (HEAD_DIM, HEAD_DIM)))

    def local(b, i, mask_columns):
        query = split(q[b, :, head(i)])
        qh[b, i], ql[b, i] = query
        scores = jnp.where(causal, dot3(query, (kh[b, i], kl[b, i]), NT), 0.0)
        scores = split(scores)
        sh[b, i], sl[b, i] = scores
        att[b, i] = dot3(scores, (vh[b, i], vl[b, i]), NN)
        t[b, :, head(i)] = gain_ref[pl.ds(c * OWN + i, 1), :] * (mask_columns * t[b, :, head(i)])

    loads[2].wait()
    loads[3].wait()
    mask_near = as_columns(mask[c, 0:1])

    def local_near(i, carry):
        local(c, i, mask_near)
        return carry

    lax.fori_loop(0, OWN, local_near, 0)
    arrived(q.at[0], INPUTS)
    arrived(k, INPUTS + 1)
    arrived(v, INPUTS + 2)
    arrived(t.at[0], INPUTS + 3)
    arrived(mask.at[0], INPUTS + 4)
    mask_far = as_columns(mask[far, 0:1])

    def kv_zero(i):
        return jnp.where(c == 0, kv[i], other[i])

    def local_far(i, carry):
        kh[far, i], kl[far, i] = split(k[:, head(i)])
        vh[far, i], vl[far, i] = split(v[:, head(i)])
        local(far, i, mask_far)
        att[1, i] = att[1, i] + dot3((qh[1, i], ql[1, i]), split(kv_zero(i)), NN)
        return carry

    lax.fori_loop(0, OWN, local_far, 0)
    for chunk in range(CHUNKS):
        scan(recv, pre, part, FORWARD, chunk, False)
    acc[...] = jnp.zeros_like(acc)

    def attend(i, carry):
        prior = split(part[rows_of(i), :])
        for b in range(2):
            row = att[b, i] + dot3((qh[b, i], ql[b, i]), prior, NN)
            att[b, i] = row
            acc[b] = acc[b] + row * row
            acc[2 + b] = acc[2 + b] + t[b, :, head(i)] * row
        return carry

    for chunk in range(CHUNKS):
        scanned(part, FORWARD, chunk)
        lax.fori_loop(chunk * BOTH, (chunk + 1) * BOTH, attend, 0, unroll=True)
    row_out[...] = jnp.zeros_like(row_out)
    for n in range(4):
        row_out[pl.ds(n, 1), :] = jnp.sum(jnp.transpose(acc[n]), axis=0, keepdims=True)
    for device in across:
        send(row_out, row_in.at[x * 2 + c], SUMS, device)
    row_in[x * 2 + c] = row_out[...]
    arrived(row_in.at[pl.ds(0, 2 * XS - 1)], SUMS)
    rows = jnp.sum(row_in[...], axis=0)
    inverse = lax.rsqrt(rows[0:2] / WIDTH + EPSILON)
    gain_dots = rows[2:4]
    slope = inverse * inverse * gain_dots / WIDTH
    inverse_columns = [as_columns(inverse[b : b + 1]) for b in range(2)]
    slope_columns = [as_columns(slope[b : b + 1]) for b in range(2)]

    def outer_qg(i, carry):
        outer = []
        for b in range(2):
            grad = inverse_columns[b] * (t[b, :, head(i)] - att[b, i] * slope_columns[b])
            g[b, i] = grad
            outer.append(dot3((qh[b, i], ql[b, i]), split(grad), TN))
        qg_one[i] = outer[1]
        comb_b[rows_of(i), :] = outer[0] + outer[1]
        return carry

    for chunk in range(CHUNKS):
        lax.fori_loop(chunk * BOTH, (chunk + 1) * BOTH, outer_qg, 0, unroll=True)
        spread(comb_b, recv_b, REVERSE, chunk)
    stat_z_out[...] = jnp.zeros_like(stat_z_out)
    stat_z_out[pl.ds(0, 1), :] = jnp.sum(inverse * gain_dots, axis=0, keepdims=True)
    stat_z_out[pl.ds(1, 1), :] = mask[0, 0:1] + mask[1, 0:1]
    for d in range(1, ZS):
        send(stat_z_out, stat_z.at[z], STAT_Z, at(y, (z + d) % ZS, c, x))
    stat_z[z] = stat_z_out[...]

    def local_grads(i, carry):
        prior = part[rows_of(i), :]
        for b in range(2):
            grad = split(g[b, i])
            query, key, value = (qh[b, i], ql[b, i]), (kh[b, i], kl[b, i]), (vh[b, i], vl[b, i])
            grad_scores = split(jnp.where(causal, dot3(grad, value, NT), 0.0))
            before = split(prior if b == 0 else prior + kv_zero(i))
            gq[b, i] = dot3(grad_scores, key, NN) + dot3(grad, before, NT)
            grad_key = dot3(grad_scores, query, TN)
            grad_value = dot3((sh[b, i], sl[b, i]), grad, TN)
            if b == 0:
                after = split(qg_one[i])
                grad_key = grad_key + dot3(value, after, NT)
                grad_value = grad_value + dot3(key, after, NN)
            gk[b, i] = grad_key
            gv[b, i] = grad_value
        return carry

    lax.fori_loop(0, OWN - 1, local_grads, 0)
    for chunk in range(CHUNKS):
        scan(recv_b, pre_b, part_b, REVERSE, chunk, True)
    arrived(stat_z.at[pl.ds(0, ZS - 1)], STAT_Z)
    stat_y_out[...] = jnp.sum(stat_z[...], axis=0)
    for d in range(1, YS):
        send(stat_y_out, stat_y.at[y], STAT_Y, at((y + d) % YS, z, c, x))
    stat_y[y] = stat_y_out[...]
    lax.fori_loop(OWN - 1, OWN, local_grads, 0)
    arrived(stat_y.at[pl.ds(0, YS - 1)], STAT_Y)
    totals = jnp.sum(stat_y[...], axis=0)
    token_total = jnp.sum(totals[1:2], axis=1, keepdims=True)
    loss_ref[...] = jnp.sum(totals[0:1], axis=1, keepdims=True) / token_total
    scale = TOKENS / token_total

    def store(vmem, hbm, i, sem):
        columns = head(c * OWN + i)
        pltpu.make_async_copy(vmem.at[c, i], hbm.at[:, columns], store_sem).start()
        send(vmem.at[far, i], hbm.at[:, columns], sem, partner)

    def scaled(i, carry):
        for b in range(2):
            gq[b, i] = gq[b, i] * scale
        store(gq, gq_hbm, i, RESULTS)
        return carry

    lax.fori_loop(0, OWN, scaled, 0)

    def last(i, carry):
        later = split(part_b[rows_of(i), :])
        for b in range(2):
            gk[b, i] = (gk[b, i] + dot3((vh[b, i], vl[b, i]), later, NT)) * scale
            gv[b, i] = (gv[b, i] + dot3((kh[b, i], kl[b, i]), later, NN)) * scale
        store(gk, gk_hbm, i, RESULTS + 1)
        store(gv, gv_hbm, i, RESULTS + 2)
        return carry

    for chunk in range(CHUNKS):
        scanned(part_b, REVERSE, chunk)
        lax.fori_loop(chunk * BOTH, (chunk + 1) * BOTH, last, 0, unroll=True)
    for base, flat in ((FORWARD, comb), (REVERSE, comb_b)):
        for chunk in range(CHUNKS):
            sent(flat.at[all_but_one], base + OUT + chunk)
            sent(flat.at[all_but_one], base + BACK + chunk)
            if base == FORWARD:
                sent(kv_far.at[pl.ds(0, BOTH)], base + PAIR + chunk)
    for n in range(4):
        sent(k, INPUTS + n)
    sent(mask.at[0], INPUTS + 4)
    sent(row_in.at[pl.ds(0, 2 * XS - 1)], SUMS)
    sent(stat_z.at[pl.ds(0, ZS - 1)], STAT_Z)
    sent(stat_y.at[pl.ds(0, YS - 1)], STAT_Y)
    for n, done in enumerate((gq, gk, gv)):
        sent(done.at[0], RESULTS + n)
        pltpu.make_async_copy(done.at[0], done.at[0], store_sem).wait()
        arrived(done.at[0], RESULTS + n)


def shards(queries, key_rows, value_rows, target, norm_gain, valid_mask):
    whole = jax.ShapeDtypeStruct(queries.shape, F32)
    full = pltpu.VMEM((HEAD_DIM, HEADS * HEAD_DIM), F32)
    half = pltpu.VMEM((HEAD_DIM, OWN * HEAD_DIM), F32)
    halves = pltpu.VMEM((2, HEAD_DIM, OWN * HEAD_DIM), F32)
    heads = pltpu.VMEM((2, OWN, HEAD_DIM, HEAD_DIM), F32)
    heads16 = pltpu.VMEM((2, OWN, HEAD_DIM, HEAD_DIM), BF16)
    states = pltpu.VMEM((OWN, HEAD_DIM, HEAD_DIM), F32)
    flat = pltpu.VMEM((OWN * HEAD_DIM, HEAD_DIM), F32)

    def tiles(count):
        return pltpu.VMEM((count, 8, HEAD_DIM), F32)

    tile = pltpu.VMEM((8, HEAD_DIM), F32)
    anywhere = pl.BlockSpec(memory_space=pl.ANY)
    vmem = pl.BlockSpec(memory_space=pltpu.VMEM)
    grad_q, grad_k, grad_v, loss = pl.pallas_call(
        kernel,
        out_shape=(whole, whole, whole, jax.ShapeDtypeStruct((1, 1), F32)),
        in_specs=[anywhere] * 4 + [vmem] * 2,
        out_specs=(anywhere, anywhere, anywhere, vmem),
        scratch_shapes=[full, full, halves, half, half, halves, tiles(2)]
        + [heads16] * 8
        + [heads] * 5
        + [pltpu.VMEM((4, HEAD_DIM, HEAD_DIM), F32)]
        + [states] * 3
        + [flat] * 4
        + [states] * 2
        + [flat] * 4
        + [tile, tiles(2 * XS), tile, tiles(ZS), tile, tiles(YS)]
        + [
            pltpu.SemaphoreType.DMA((4,)),
            pltpu.SemaphoreType.DMA,
            pltpu.SemaphoreType.DMA((COUNT,)),
            pltpu.SemaphoreType.DMA((COUNT,)),
        ],
        compiler_params=pltpu.CompilerParams(collective_id=0, has_side_effects=True),
        name="linear_attention",
    )(
        queries, key_rows, value_rows, target,
        norm_gain.reshape(HEADS, HEAD_DIM), valid_mask.reshape(1, HEAD_DIM),
    )
    return grad_q, grad_k, grad_v, loss.reshape(())


def solution(mesh):
    return jax.shard_map(
        shards,
        mesh=mesh,
        in_specs=(P("seq", "head"),) * 4 + (P("head"), P("seq")),
        out_specs=(P("seq", "head"),) * 3 + (P(),),
        check_vma=False,
    )
```

```python
import jax
import jax.numpy as jnp
from jax import lax
from jax.experimental import pallas as pl
from jax.experimental.pallas import tpu as pltpu
from jax.sharding import PartitionSpec as P

HEAD_DIM = 128
WIDTH = 4096
TOKENS = 8192
HEADS = 8
OWN = 4
CHUNKS = 2
BOTH = OWN // CHUNKS
YS, ZS, XS = 4, 8, 4
CHIPS = YS * ZS
CHUNK_ROWS = BOTH * HEAD_DIM
ROWS = CHUNK_ROWS // CHIPS
EPSILON = 1e-06
VMEM_LIMIT = 24 * 2**20

F32 = jnp.float32
BF16 = jnp.bfloat16
MESH = pl.DeviceIdType.MESH
PAIR, OUT, BACK = 0, CHUNKS, 2 * CHUNKS
FORWARD, REVERSE, INPUTS = 0, 3 * CHUNKS, 6 * CHUNKS
SUMS, STAT_Z, STAT_Y, RESULTS, COUNT = INPUTS + 5, INPUTS + 6, INPUTS + 7, INPUTS + 8, INPUTS + 11


def ring(delta, count):
    return min(delta, count - delta)


OFFSETS = sorted(
    ((dy, dz) for dy in range(YS) for dz in range(ZS) if dy or dz),
    key=lambda o: -(ring(o[0], YS) + ring(o[1], ZS)),
)


def split(x):
    high = x.astype(BF16)
    return high, (x - high.astype(F32)).astype(BF16)


def dot3(a, b, contract):
    dims = ((contract[:1], contract[1:]), ((), ()))

    def one(x, y):
        return lax.dot_general(x, y, dims, preferred_element_type=F32)

    return one(a[0], b[0]) + (one(a[0], b[1]) + one(a[1], b[0]))


NN, NT, TN = (1, 0), (1, 1), (0, 0)


def kernel(
    q_hbm, k_hbm, v_hbm, t_hbm, gain_hbm, mask_hbm,
    gq_out, gk_out, gv_out, loss_hbm,
    k_all, v_all, q, k, v, t, gain, mask_row, mask, loss,
    qh, ql, kh, kl, vh, vl, sh, sl, att, g, gq, gk, gv, acc,
    kv, kv_far, other, comb, recv, pre, part,
    qg, qg_one, comb_b, recv_b, pre_b, part_b,
    row_out, row_in, stat_z_out, stat_z, stat_y_out, stat_y,
    load_sems, send_sems, recv_sems,
):
    s, x = lax.axis_index("seq"), lax.axis_index("head")
    y, z, c = s // 16, (s // 2) % ZS, s % 2
    me = y * ZS + z
    far = 1 - c

    def at(ty, tz, tc, tx):
        return (ty * 16 + tz * 2 + tc, tx)

    partner = at(y, z, far, x)
    chips = [((y + dy) % YS, (z + dz) % ZS) for dy, dz in OFFSETS]
    across = [at(y, z, tc, (x + d) % XS) for d in (2, 1, 3) for tc in range(2)] + [partner]
    greeted = [at(ty, tz, c, x) for ty, tz in chips] + across
    def heads_of(core):
        return pl.ds(pl.multiple_of(core * OWN * HEAD_DIM, HEAD_DIM), OWN * HEAD_DIM)

    def head(i):
        return pl.ds(pl.multiple_of(i * HEAD_DIM, HEAD_DIM), HEAD_DIM)

    loads = [
        pltpu.make_async_copy(k_hbm, k_all, load_sems.at[0]),
        pltpu.make_async_copy(v_hbm, v_all, load_sems.at[1]),
        pltpu.make_async_copy(q_hbm.at[:, heads_of(c)], q.at[c], load_sems.at[2]),
        pltpu.make_async_copy(t_hbm.at[:, heads_of(c)], t.at[c], load_sems.at[3]),
        pltpu.make_async_copy(gain_hbm, gain, load_sems.at[4]),
        pltpu.make_async_copy(mask_hbm, mask_row, load_sems.at[5]),
    ]
    for copy in loads:
        copy.start()

    barrier = pltpu.get_barrier_semaphore()
    for device in greeted:
        pl.semaphore_signal(barrier, inc=1, device_id=device, device_id_type=MESH)

    def send(src, dst, sem, device):
        pltpu.make_async_remote_copy(
            src_ref=src, dst_ref=dst, send_sem=send_sems.at[sem], recv_sem=recv_sems.at[sem],
            device_id=device, device_id_type=MESH,
        ).start()

    def arrived(ref, sem):
        pltpu.make_async_copy(ref, ref, recv_sems.at[sem]).wait()

    def sent(ref, sem):
        pltpu.make_async_copy(ref, ref, send_sems.at[sem]).wait()

    def piece(chunk, i):
        return pl.ds(pl.multiple_of(chunk * CHUNK_ROWS + i * ROWS, ROWS), ROWS)

    all_but_one = pl.ds(0, (CHIPS - 1) * ROWS)

    def rows_of(i):
        return pl.ds(pl.multiple_of(i * HEAD_DIM, HEAD_DIM), HEAD_DIM)

    def spread(comb, recv, base, chunk):
        for ty, tz in chips:
            send(comb.at[piece(chunk, ty * ZS + tz)], recv.at[piece(chunk, me)], base + OUT + chunk, at(ty, tz, c, x))
        recv[piece(chunk, me), :] = comb[piece(chunk, me), :]

    def scan(recv, pre, part, base, chunk, reverse):
        arrived(recv.at[all_but_one], base + OUT + chunk)
        total = jnp.zeros((ROWS, HEAD_DIM), F32)
        for i in reversed(range(CHIPS)) if reverse else range(CHIPS):
            pre[piece(chunk, i), :] = total
            total = total + recv[piece(chunk, i), :]
        for ty, tz in chips:
            send(pre.at[piece(chunk, ty * ZS + tz)], part.at[piece(chunk, me)], base + BACK + chunk, at(ty, tz, c, x))
        part[piece(chunk, me), :] = pre[piece(chunk, me), :]

    def scanned(part, base, chunk):
        arrived(part.at[all_but_one], base + BACK + chunk)

    loads[0].wait()
    loads[1].wait()

    def outer_far(i, carry):
        columns = head(far * OWN + i)
        kv_far[i] = dot3(split(k_all[:, columns]), split(v_all[:, columns]), TN)
        return carry

    def outer_own(i, carry):
        columns = head(c * OWN + i)
        key, value = split(k_all[:, columns]), split(v_all[:, columns])
        kh[c, i], kl[c, i] = key
        vh[c, i], vl[c, i] = value
        kv[i] = dot3(key, value, TN)
        return carry

    lax.fori_loop(0, OWN, outer_far, 0, unroll=2)
    lax.fori_loop(0, OWN, outer_own, 0, unroll=2)
    pl.semaphore_wait(barrier, len(greeted))
    for chunk in range(CHUNKS):
        half = pl.ds(chunk * BOTH, BOTH)
        send(kv_far.at[half], other.at[half], FORWARD + PAIR + chunk, partner)
    for chunk in range(CHUNKS):
        arrived(other.at[pl.ds(0, BOTH)], FORWARD + PAIR + chunk)
        for i in range(chunk * BOTH, (chunk + 1) * BOTH):
            comb[rows_of(i), :] = kv[i] + other[i]
        spread(comb, recv, FORWARD, chunk)

    send(q_hbm.at[:, heads_of(far)], q.at[c], INPUTS, partner)
    send(k_hbm.at[:, heads_of(far)], k, INPUTS + 1, partner)
    send(v_hbm.at[:, heads_of(far)], v, INPUTS + 2, partner)
    send(t_hbm.at[:, heads_of(far)], t.at[c], INPUTS + 3, partner)
    loads[4].wait()
    loads[5].wait()
    mask[c] = jnp.broadcast_to(mask_row[...].astype(F32), (8, HEAD_DIM))
    send(mask.at[c], mask.at[c], INPUTS + 4, partner)

    token = lax.broadcasted_iota(jnp.int32, (HEAD_DIM, HEAD_DIM), 0)
    column = lax.broadcasted_iota(jnp.int32, (HEAD_DIM, HEAD_DIM), 1)
    causal = token >= column

    def as_columns(row):
        return jnp.transpose(jnp.broadcast_to(row, (HEAD_DIM, HEAD_DIM)))

    def local(b, i, mask_columns):
        query = split(q[b, :, head(i)])
        qh[b, i], ql[b, i] = query
        scores = jnp.where(causal, dot3(query, (kh[b, i], kl[b, i]), NT), 0.0)
        scores = split(scores)
        sh[b, i], sl[b, i] = scores
        att[b, i] = dot3(scores, (vh[b, i], vl[b, i]), NN)
        t[b, :, head(i)] = gain[pl.ds(c * OWN + i, 1), :] * (mask_columns * t[b, :, head(i)])

    loads[2].wait()
    loads[3].wait()
    mask_near = as_columns(mask[c, 0:1])

    def local_near(i, carry):
        local(c, i, mask_near)
        return carry

    lax.fori_loop(0, OWN, local_near, 0)
    arrived(q.at[0], INPUTS)
    arrived(k, INPUTS + 1)
    arrived(v, INPUTS + 2)
    arrived(t.at[0], INPUTS + 3)
    arrived(mask.at[0], INPUTS + 4)
    mask_far = as_columns(mask[far, 0:1])

    def kv_zero(i):
        return jnp.where(c == 0, kv[i], other[i])

    def local_far(i, carry):
        kh[far, i], kl[far, i] = split(k[:, head(i)])
        vh[far, i], vl[far, i] = split(v[:, head(i)])
        local(far, i, mask_far)
        att[1, i] = att[1, i] + dot3((qh[1, i], ql[1, i]), split(kv_zero(i)), NN)
        return carry

    lax.fori_loop(0, OWN, local_far, 0)
    for chunk in range(CHUNKS):
        scan(recv, pre, part, FORWARD, chunk, False)
    acc[...] = jnp.zeros_like(acc)

    def attend(i, carry):
        prior = split(part[rows_of(i), :])
        for b in range(2):
            row = att[b, i] + dot3((qh[b, i], ql[b, i]), prior, NN)
            att[b, i] = row
            acc[b] = acc[b] + row * row
            acc[2 + b] = acc[2 + b] + t[b, :, head(i)] * row
        return carry

    for chunk in range(CHUNKS):
        scanned(part, FORWARD, chunk)
        lax.fori_loop(chunk * BOTH, (chunk + 1) * BOTH, attend, 0, unroll=True)
    row_out[...] = jnp.zeros_like(row_out)
    for n in range(4):
        row_out[pl.ds(n, 1), :] = jnp.sum(jnp.transpose(acc[n]), axis=0, keepdims=True)
    for device in across:
        send(row_out, row_in.at[x * 2 + c], SUMS, device)
    row_in[x * 2 + c] = row_out[...]
    arrived(row_in.at[pl.ds(0, 2 * XS - 1)], SUMS)
    rows = jnp.sum(row_in[...], axis=0)
    inverse = lax.rsqrt(rows[0:2] / WIDTH + EPSILON)
    gain_dots = rows[2:4]
    slope = inverse * inverse * gain_dots / WIDTH
    stat_z_out[...] = jnp.zeros_like(stat_z_out)
    stat_z_out[pl.ds(0, 1), :] = jnp.sum(inverse * gain_dots, axis=0, keepdims=True)
    stat_z_out[pl.ds(1, 1), :] = mask[0, 0:1] + mask[1, 0:1]
    for d in range(1, ZS):
        send(stat_z_out, stat_z.at[z], STAT_Z, at(y, (z + d) % ZS, c, x))
    stat_z[z] = stat_z_out[...]
    inverse_columns = [as_columns(inverse[b : b + 1]) for b in range(2)]
    slope_columns = [as_columns(slope[b : b + 1]) for b in range(2)]

    def outer_qg(i, carry):
        outer = []
        for b in range(2):
            grad = inverse_columns[b] * (t[b, :, head(i)] - att[b, i] * slope_columns[b])
            g[b, i] = grad
            outer.append(dot3((qh[b, i], ql[b, i]), split(grad), TN))
        qg_one[i] = outer[1]
        comb_b[rows_of(i), :] = outer[0] + outer[1]
        return carry

    for chunk in range(CHUNKS):
        lax.fori_loop(chunk * BOTH, (chunk + 1) * BOTH, outer_qg, 0, unroll=True)
        spread(comb_b, recv_b, REVERSE, chunk)
    def local_grads(i, carry):
        prior = part[rows_of(i), :]
        for b in range(2):
            grad = split(g[b, i])
            query, key, value = (qh[b, i], ql[b, i]), (kh[b, i], kl[b, i]), (vh[b, i], vl[b, i])
            grad_scores = split(jnp.where(causal, dot3(grad, value, NT), 0.0))
            before = split(prior if b == 0 else prior + kv_zero(i))
            gq[b, i] = dot3(grad_scores, key, NN) + dot3(grad, before, NT)
            grad_key = dot3(grad_scores, query, TN)
            grad_value = dot3((sh[b, i], sl[b, i]), grad, TN)
            if b == 0:
                after = split(qg_one[i])
                grad_key = grad_key + dot3(value, after, NT)
                grad_value = grad_value + dot3(key, after, NN)
            gk[b, i] = grad_key
            gv[b, i] = grad_value
        return carry

    lax.fori_loop(0, OWN, local_grads, 0)
    arrived(stat_z.at[pl.ds(0, ZS - 1)], STAT_Z)
    stat_y_out[...] = jnp.sum(stat_z[...], axis=0)
    for d in range(1, YS):
        send(stat_y_out, stat_y.at[y], STAT_Y, at((y + d) % YS, z, c, x))
    stat_y[y] = stat_y_out[...]
    for chunk in range(CHUNKS):
        scan(recv_b, pre_b, part_b, REVERSE, chunk, True)
    arrived(stat_y.at[pl.ds(0, YS - 1)], STAT_Y)
    totals = jnp.sum(stat_y[...], axis=0)
    token_total = jnp.sum(totals[1:2], axis=1, keepdims=True)
    loss[...] = jnp.sum(totals[0:1], axis=1, keepdims=True) / token_total
    out_loss = pltpu.make_async_copy(loss, loss_hbm, load_sems.at[6])
    out_loss.start()
    scale = TOKENS / token_total

    def store(block, out, i, sem, finished):
        columns = head(c * OWN + i)
        block[far, i] = finished(far)
        send(block.at[far, i], out.at[:, columns], sem, partner)
        out[:, columns] = finished(c)

    def scaled(i, carry):
        store(gq, gq_out, i, RESULTS, lambda b: gq[b, i] * scale)
        return carry

    lax.fori_loop(0, OWN, scaled, 0)

    def last(i, carry):
        later = split(part_b[rows_of(i), :])
        store(gk, gk_out, i, RESULTS + 1, lambda b: (gk[b, i] + dot3((vh[b, i], vl[b, i]), later, NT)) * scale)
        store(gv, gv_out, i, RESULTS + 2, lambda b: (gv[b, i] + dot3((kh[b, i], kl[b, i]), later, NN)) * scale)
        return carry

    for chunk in range(CHUNKS):
        scanned(part_b, REVERSE, chunk)
        lax.fori_loop(chunk * BOTH, (chunk + 1) * BOTH, last, 0, unroll=True)
    for base, flat in ((FORWARD, comb), (REVERSE, comb_b)):
        for chunk in range(CHUNKS):
            sent(flat.at[all_but_one], base + OUT + chunk)
            sent(flat.at[all_but_one], base + BACK + chunk)
            if base == FORWARD:
                sent(kv_far.at[pl.ds(0, BOTH)], base + PAIR + chunk)
    for n in range(4):
        sent(k, INPUTS + n)
    sent(mask.at[0], INPUTS + 4)
    sent(row_in.at[pl.ds(0, 2 * XS - 1)], SUMS)
    sent(stat_z.at[pl.ds(0, ZS - 1)], STAT_Z)
    sent(stat_y.at[pl.ds(0, YS - 1)], STAT_Y)
    for n, done in enumerate((gq, gk, gv)):
        sent(done.at[0], RESULTS + n)
        arrived(done.at[0], RESULTS + n)
    out_loss.wait()


def hand_out(*refs):
    given, outs, sems = refs[:3], refs[3:6], refs[6]
    copies = [pltpu.make_async_copy(given[n], outs[n], sems.at[n]) for n in range(3)]
    for copy in copies:
        copy.start()
    for copy in copies:
        copy.wait()


def shards(queries, key_rows, value_rows, target, norm_gain, valid_mask):
    whole = jax.ShapeDtypeStruct(queries.shape, F32)
    full = pltpu.VMEM((HEAD_DIM, HEADS * HEAD_DIM), F32)
    half = pltpu.VMEM((HEAD_DIM, OWN * HEAD_DIM), F32)
    halves = pltpu.VMEM((2, HEAD_DIM, OWN * HEAD_DIM), F32)
    heads = pltpu.VMEM((2, OWN, HEAD_DIM, HEAD_DIM), F32)
    heads16 = pltpu.VMEM((2, OWN, HEAD_DIM, HEAD_DIM), BF16)
    states = pltpu.VMEM((OWN, HEAD_DIM, HEAD_DIM), F32)
    flat = pltpu.VMEM((OWN * HEAD_DIM, HEAD_DIM), F32)

    def tiles(count):
        return pltpu.VMEM((count, 8, HEAD_DIM), F32)

    tile = pltpu.VMEM((8, HEAD_DIM), F32)
    anywhere = pl.BlockSpec(memory_space=pltpu.HBM)
    vmem = pl.BlockSpec(memory_space=pltpu.VMEM)
    arrays = (queries, key_rows, value_rows, target)
    arrays += (norm_gain.reshape(HEADS, HEAD_DIM), valid_mask.reshape(1, HEAD_DIM))
    grad_q, grad_k, grad_v, loss = pl.pallas_call(
        kernel,
        out_shape=(whole, whole, whole, jax.ShapeDtypeStruct((1, 1), F32)),
        in_specs=[anywhere] * 6,
        out_specs=(vmem, vmem, vmem, anywhere),
        scratch_shapes=[full, full, halves, half, half, halves, tile, pltpu.VMEM((1, HEAD_DIM), jnp.int32), tiles(2)]
        + [pltpu.VMEM((1, 1), F32)]
        + [heads16] * 8
        + [heads] * 5
        + [pltpu.VMEM((4, HEAD_DIM, HEAD_DIM), F32)]
        + [states] * 3
        + [flat] * 4
        + [states] * 2
        + [flat] * 4
        + [tile, tiles(2 * XS), tile, tiles(ZS), tile, tiles(YS)]
        + [
            pltpu.SemaphoreType.DMA((7,)),
            pltpu.SemaphoreType.DMA((COUNT,)),
            pltpu.SemaphoreType.DMA((COUNT,)),
        ],
        compiler_params=pltpu.CompilerParams(
            collective_id=0, has_side_effects=True, vmem_limit_bytes=VMEM_LIMIT
        ),
        name="linear_attention",
    )(
        *[pltpu.with_memory_space_constraint(array, pltpu.HBM) for array in arrays],
    )
    grad_q, grad_k, grad_v = pl.pallas_call(
        hand_out,
        out_shape=(whole,) * 3,
        in_specs=[vmem] * 3,
        out_specs=(anywhere,) * 3,
        scratch_shapes=[pltpu.SemaphoreType.DMA((3,))],
        compiler_params=pltpu.CompilerParams(vmem_limit_bytes=4 * 2**20),
        name="hand_out",
    )(grad_q, grad_k, grad_v)
    return grad_q, grad_k, grad_v, loss.reshape(())


def solution(mesh):
    return jax.shard_map(
        shards,
        mesh=mesh,
        in_specs=(P("seq", "head"),) * 4 + (P("head"), P("seq")),
        out_specs=(P("seq", "head"),) * 3 + (P(),),
        check_vma=False,
    )
```

```python
import jax
import jax.numpy as jnp
from jax import lax
from jax.experimental import pallas as pl
from jax.experimental.pallas import tpu as pltpu
from jax.sharding import PartitionSpec as P

HEAD_DIM = 128
WIDTH = 4096
TOKENS = 8192
HEADS = 8
OWN = 4
CHUNKS = 2
BOTH = OWN // CHUNKS
YS, ZS, XS = 4, 8, 4
CHIPS = YS * ZS
CHUNK_ROWS = BOTH * HEAD_DIM
ROWS = CHUNK_ROWS // CHIPS
EPSILON = 1e-06
VMEM_LIMIT = 24 * 2**20

F32 = jnp.float32
BF16 = jnp.bfloat16
MESH = pl.DeviceIdType.MESH
PAIR, OUT, BACK = 0, CHUNKS, 2 * CHUNKS
FORWARD, REVERSE, INPUTS = 0, 3 * CHUNKS, 6 * CHUNKS
SUMS, STAT_Z, STAT_Y, RESULTS, COUNT = INPUTS + 5, INPUTS + 6, INPUTS + 7, INPUTS + 8, INPUTS + 11


def ring(delta, count):
    return min(delta, count - delta)


OFFSETS = sorted(
    ((dy, dz) for dy in range(YS) for dz in range(ZS) if dy or dz),
    key=lambda o: -(ring(o[0], YS) + ring(o[1], ZS)),
)


def split(x):
    high = x.astype(BF16)
    return high, (x - high.astype(F32)).astype(BF16)


def dot3(a, b, contract):
    dims = ((contract[:1], contract[1:]), ((), ()))

    def one(x, y):
        return lax.dot_general(x, y, dims, preferred_element_type=F32)

    return one(a[0], b[0]) + (one(a[0], b[1]) + one(a[1], b[0]))


NN, NT, TN = (1, 0), (1, 1), (0, 0)


def kernel(
    q_hbm, k_hbm, v_hbm, t_hbm, gain_hbm, mask_hbm,
    gq_out, gk_out, gv_out, loss_out,
    k_all, v_all, q, k, v, t, gain, mask_row, mask,
    qh, ql, kh, kl, vh, vl, sh, sl, att, g, gq, gk, gv, acc,
    kv, kv_far, other, comb, recv, pre, part,
    qg, qg_one, comb_b, recv_b, pre_b, part_b,
    row_out, row_in, stat_z_out, stat_z, stat_y_out, stat_y,
    load_sems, store_sem, send_sems, recv_sems,
):
    s, x = lax.axis_index("seq"), lax.axis_index("head")
    y, z, c = s // 16, (s // 2) % ZS, s % 2
    me = y * ZS + z
    far = 1 - c

    def at(ty, tz, tc, tx):
        return (ty * 16 + tz * 2 + tc, tx)

    partner = at(y, z, far, x)
    chips = [((y + dy) % YS, (z + dz) % ZS) for dy, dz in OFFSETS]
    across = [at(y, z, tc, (x + d) % XS) for d in (2, 1, 3) for tc in range(2)] + [partner]
    greeted = [at(ty, tz, c, x) for ty, tz in chips] + across
    def heads_of(core):
        return pl.ds(pl.multiple_of(core * OWN * HEAD_DIM, HEAD_DIM), OWN * HEAD_DIM)

    def head(i):
        return pl.ds(pl.multiple_of(i * HEAD_DIM, HEAD_DIM), HEAD_DIM)

    loads = [
        pltpu.make_async_copy(k_hbm, k_all, load_sems.at[0]),
        pltpu.make_async_copy(v_hbm, v_all, load_sems.at[1]),
        pltpu.make_async_copy(q_hbm.at[:, heads_of(c)], q.at[c], load_sems.at[2]),
        pltpu.make_async_copy(t_hbm.at[:, heads_of(c)], t.at[c], load_sems.at[3]),
        pltpu.make_async_copy(gain_hbm, gain, load_sems.at[4]),
        pltpu.make_async_copy(mask_hbm, mask_row, load_sems.at[5]),
    ]
    for copy in loads:
        copy.start()

    barrier = pltpu.get_barrier_semaphore()
    for device in greeted:
        pl.semaphore_signal(barrier, inc=1, device_id=device, device_id_type=MESH)

    def send(src, dst, sem, device):
        pltpu.make_async_remote_copy(
            src_ref=src, dst_ref=dst, send_sem=send_sems.at[sem], recv_sem=recv_sems.at[sem],
            device_id=device, device_id_type=MESH,
        ).start()

    def arrived(ref, sem):
        pltpu.make_async_copy(ref, ref, recv_sems.at[sem]).wait()

    def sent(ref, sem):
        pltpu.make_async_copy(ref, ref, send_sems.at[sem]).wait()

    def piece(chunk, i):
        return pl.ds(pl.multiple_of(chunk * CHUNK_ROWS + i * ROWS, ROWS), ROWS)

    all_but_one = pl.ds(0, (CHIPS - 1) * ROWS)

    def rows_of(i):
        return pl.ds(pl.multiple_of(i * HEAD_DIM, HEAD_DIM), HEAD_DIM)

    def spread(comb, recv, base, chunk):
        for ty, tz in chips:
            send(comb.at[piece(chunk, ty * ZS + tz)], recv.at[piece(chunk, me)], base + OUT + chunk, at(ty, tz, c, x))
        recv[piece(chunk, me), :] = comb[piece(chunk, me), :]

    def scan(recv, pre, part, base, chunk, reverse):
        arrived(recv.at[all_but_one], base + OUT + chunk)
        total = jnp.zeros((ROWS, HEAD_DIM), F32)
        for i in reversed(range(CHIPS)) if reverse else range(CHIPS):
            pre[piece(chunk, i), :] = total
            total = total + recv[piece(chunk, i), :]
        for ty, tz in chips:
            send(pre.at[piece(chunk, ty * ZS + tz)], part.at[piece(chunk, me)], base + BACK + chunk, at(ty, tz, c, x))
        part[piece(chunk, me), :] = pre[piece(chunk, me), :]

    def scanned(part, base, chunk):
        arrived(part.at[all_but_one], base + BACK + chunk)

    loads[0].wait()
    loads[1].wait()

    def outer_far(i, carry):
        columns = head(far * OWN + i)
        kv_far[i] = dot3(split(k_all[:, columns]), split(v_all[:, columns]), TN)
        return carry

    def outer_own(i, carry):
        columns = head(c * OWN + i)
        key, value = split(k_all[:, columns]), split(v_all[:, columns])
        kh[c, i], kl[c, i] = key
        vh[c, i], vl[c, i] = value
        kv[i] = dot3(key, value, TN)
        return carry

    lax.fori_loop(0, OWN, outer_far, 0, unroll=2)
    lax.fori_loop(0, OWN, outer_own, 0, unroll=2)
    pl.semaphore_wait(barrier, len(greeted))
    for chunk in range(CHUNKS):
        half = pl.ds(chunk * BOTH, BOTH)
        send(kv_far.at[half], other.at[half], FORWARD + PAIR + chunk, partner)
    for chunk in range(CHUNKS):
        arrived(other.at[pl.ds(0, BOTH)], FORWARD + PAIR + chunk)
        for i in range(chunk * BOTH, (chunk + 1) * BOTH):
            comb[rows_of(i), :] = kv[i] + other[i]
        spread(comb, recv, FORWARD, chunk)

    send(q_hbm.at[:, heads_of(far)], q.at[c], INPUTS, partner)
    send(k_hbm.at[:, heads_of(far)], k, INPUTS + 1, partner)
    send(v_hbm.at[:, heads_of(far)], v, INPUTS + 2, partner)
    send(t_hbm.at[:, heads_of(far)], t.at[c], INPUTS + 3, partner)
    loads[4].wait()
    loads[5].wait()
    mask[c] = jnp.broadcast_to(mask_row[...].astype(F32), (8, HEAD_DIM))
    send(mask.at[c], mask.at[c], INPUTS + 4, partner)

    token = lax.broadcasted_iota(jnp.int32, (HEAD_DIM, HEAD_DIM), 0)
    column = lax.broadcasted_iota(jnp.int32, (HEAD_DIM, HEAD_DIM), 1)
    causal = token >= column

    def as_columns(row):
        return jnp.transpose(jnp.broadcast_to(row, (HEAD_DIM, HEAD_DIM)))

    def local(b, i, mask_columns):
        query = split(q[b, :, head(i)])
        qh[b, i], ql[b, i] = query
        scores = jnp.where(causal, dot3(query, (kh[b, i], kl[b, i]), NT), 0.0)
        scores = split(scores)
        sh[b, i], sl[b, i] = scores
        att[b, i] = dot3(scores, (vh[b, i], vl[b, i]), NN)
        t[b, :, head(i)] = gain[pl.ds(c * OWN + i, 1), :] * (mask_columns * t[b, :, head(i)])

    loads[2].wait()
    loads[3].wait()
    mask_near = as_columns(mask[c, 0:1])

    def local_near(i, carry):
        local(c, i, mask_near)
        return carry

    lax.fori_loop(0, OWN, local_near, 0)
    arrived(q.at[0], INPUTS)
    arrived(k, INPUTS + 1)
    arrived(v, INPUTS + 2)
    arrived(t.at[0], INPUTS + 3)
    arrived(mask.at[0], INPUTS + 4)
    mask_far = as_columns(mask[far, 0:1])

    def kv_zero(i):
        return jnp.where(c == 0, kv[i], other[i])

    def local_far(i, carry):
        kh[far, i], kl[far, i] = split(k[:, head(i)])
        vh[far, i], vl[far, i] = split(v[:, head(i)])
        local(far, i, mask_far)
        att[1, i] = att[1, i] + dot3((qh[1, i], ql[1, i]), split(kv_zero(i)), NN)
        return carry

    lax.fori_loop(0, OWN, local_far, 0)
    for chunk in range(CHUNKS):
        scan(recv, pre, part, FORWARD, chunk, False)
    acc[...] = jnp.zeros_like(acc)

    def stacked(high, low, i):
        return [part_of[:, i].reshape(2 * HEAD_DIM, HEAD_DIM) for part_of in (high, low)]

    def attend(i, carry):
        prior = split(part[rows_of(i), :])
        both = dot3(stacked(qh, ql, i), prior, NN)
        for b in range(2):
            row = att[b, i] + both[b * HEAD_DIM : (b + 1) * HEAD_DIM]
            att[b, i] = row
            acc[b] = acc[b] + row * row
            acc[2 + b] = acc[2 + b] + t[b, :, head(i)] * row
        return carry

    for chunk in range(CHUNKS):
        scanned(part, FORWARD, chunk)
        lax.fori_loop(chunk * BOTH, (chunk + 1) * BOTH, attend, 0, unroll=True)
    row_out[...] = jnp.zeros_like(row_out)
    for n in range(4):
        row_out[pl.ds(n, 1), :] = jnp.sum(jnp.transpose(acc[n]), axis=0, keepdims=True)
    for device in across:
        send(row_out, row_in.at[x * 2 + c], SUMS, device)
    row_in[x * 2 + c] = row_out[...]
    arrived(row_in.at[pl.ds(0, 2 * XS - 1)], SUMS)
    rows = jnp.sum(row_in[...], axis=0)
    inverse = lax.rsqrt(rows[0:2] / WIDTH + EPSILON)
    gain_dots = rows[2:4]
    slope = inverse * inverse * gain_dots / WIDTH
    stat_z_out[...] = jnp.zeros_like(stat_z_out)
    stat_z_out[pl.ds(0, 1), :] = jnp.sum(inverse * gain_dots, axis=0, keepdims=True)
    stat_z_out[pl.ds(1, 1), :] = mask[0, 0:1] + mask[1, 0:1]
    for d in range(1, ZS):
        send(stat_z_out, stat_z.at[z], STAT_Z, at(y, (z + d) % ZS, c, x))
    stat_z[z] = stat_z_out[...]
    inverse_columns = [as_columns(inverse[b : b + 1]) for b in range(2)]
    slope_columns = [as_columns(slope[b : b + 1]) for b in range(2)]

    def outer_qg(i, carry):
        outer = []
        for b in range(2):
            grad = inverse_columns[b] * (t[b, :, head(i)] - att[b, i] * slope_columns[b])
            g[b, i] = grad
            outer.append(dot3((qh[b, i], ql[b, i]), split(grad), TN))
        qg_one[i] = outer[1]
        comb_b[rows_of(i), :] = outer[0] + outer[1]
        return carry

    for chunk in range(CHUNKS):
        lax.fori_loop(chunk * BOTH, (chunk + 1) * BOTH, outer_qg, 0, unroll=True)
        spread(comb_b, recv_b, REVERSE, chunk)
    def local_grads(i, carry):
        prior = part[rows_of(i), :]
        for b in range(2):
            grad = split(g[b, i])
            query, key, value = (qh[b, i], ql[b, i]), (kh[b, i], kl[b, i]), (vh[b, i], vl[b, i])
            grad_scores = split(jnp.where(causal, dot3(grad, value, NT), 0.0))
            before = split(prior if b == 0 else prior + kv_zero(i))
            gq[b, i] = dot3(grad_scores, key, NN) + dot3(grad, before, NT)
            grad_key = dot3(grad_scores, query, TN)
            grad_value = dot3((sh[b, i], sl[b, i]), grad, TN)
            if b == 0:
                after = split(qg_one[i])
                grad_key = grad_key + dot3(value, after, NT)
                grad_value = grad_value + dot3(key, after, NN)
            gk[b, i] = grad_key
            gv[b, i] = grad_value
        return carry

    lax.fori_loop(0, OWN, local_grads, 0)
    arrived(stat_z.at[pl.ds(0, ZS - 1)], STAT_Z)
    stat_y_out[...] = jnp.sum(stat_z[...], axis=0)
    for d in range(1, YS):
        send(stat_y_out, stat_y.at[y], STAT_Y, at((y + d) % YS, z, c, x))
    stat_y[y] = stat_y_out[...]
    for chunk in range(CHUNKS):
        scan(recv_b, pre_b, part_b, REVERSE, chunk, True)
    arrived(stat_y.at[pl.ds(0, YS - 1)], STAT_Y)
    totals = jnp.sum(stat_y[...], axis=0)
    token_total = jnp.sum(totals[1:2], axis=1, keepdims=True)
    loss_out[...] = jnp.broadcast_to(jnp.sum(totals[0:1], axis=1, keepdims=True) / token_total, loss_out.shape)
    scale = TOKENS / token_total

    def store(block, out, i, sem):
        columns = head(c * OWN + i)
        send(block.at[far, i], out.at[:, columns], sem, partner)
        pltpu.make_async_copy(block.at[c, i], out.at[:, columns], store_sem).start()

    def scaled(i, carry):
        for b in range(2):
            gq[b, i] = gq[b, i] * scale
        store(gq, gq_out, i, RESULTS)
        return carry

    lax.fori_loop(0, OWN, scaled, 0)

    def last(chunk):
        for i in range(chunk * BOTH, (chunk + 1) * BOTH):
            later = split(part_b[rows_of(i), :])
            grad_keys = [gk[b, i] + dot3((vh[b, i], vl[b, i]), later, NT) for b in range(2)]
            grad_values = [gv[b, i] + dot3((kh[b, i], kl[b, i]), later, NN) for b in range(2)]
            for b in range(2):
                gk[b, i] = grad_keys[b] * scale
                gv[b, i] = grad_values[b] * scale
            store(gk, gk_out, i, RESULTS + 1)
            store(gv, gv_out, i, RESULTS + 2)

    for chunk in range(CHUNKS):
        scanned(part_b, REVERSE, chunk)
        last(chunk)
    for base, flat in ((FORWARD, comb), (REVERSE, comb_b)):
        for chunk in range(CHUNKS):
            sent(flat.at[all_but_one], base + OUT + chunk)
            sent(flat.at[all_but_one], base + BACK + chunk)
            if base == FORWARD:
                sent(kv_far.at[pl.ds(0, BOTH)], base + PAIR + chunk)
    for n in range(4):
        sent(k, INPUTS + n)
    sent(mask.at[0], INPUTS + 4)
    sent(row_in.at[pl.ds(0, 2 * XS - 1)], SUMS)
    sent(stat_z.at[pl.ds(0, ZS - 1)], STAT_Z)
    sent(stat_y.at[pl.ds(0, YS - 1)], STAT_Y)
    for n, done in enumerate((gq, gk, gv)):
        sent(done.at[0], RESULTS + n)
        pltpu.make_async_copy(done.at[0], done.at[0], store_sem).wait()
        arrived(done.at[0], RESULTS + n)


def hand_out(*refs):
    given, outs, sems, loss = refs[:4], refs[4:8], refs[8], refs[9]
    loss[...] = given[3][0:1, 0:1]
    copies = [pltpu.make_async_copy(loss, outs[3], sems.at[3])]
    copies += [pltpu.make_async_copy(given[n], outs[n], sems.at[n]) for n in range(3)]
    for copy in copies:
        copy.start()
    for copy in copies:
        copy.wait()


def shards(queries, key_rows, value_rows, target, norm_gain, valid_mask):
    whole = jax.ShapeDtypeStruct(queries.shape, F32)
    full = pltpu.VMEM((HEAD_DIM, HEADS * HEAD_DIM), F32)
    half = pltpu.VMEM((HEAD_DIM, OWN * HEAD_DIM), F32)
    halves = pltpu.VMEM((2, HEAD_DIM, OWN * HEAD_DIM), F32)
    heads = pltpu.VMEM((2, OWN, HEAD_DIM, HEAD_DIM), F32)
    heads16 = pltpu.VMEM((2, OWN, HEAD_DIM, HEAD_DIM), BF16)
    states = pltpu.VMEM((OWN, HEAD_DIM, HEAD_DIM), F32)
    flat = pltpu.VMEM((OWN * HEAD_DIM, HEAD_DIM), F32)

    def tiles(count):
        return pltpu.VMEM((count, 8, HEAD_DIM), F32)

    tile = pltpu.VMEM((8, HEAD_DIM), F32)
    anywhere = pl.BlockSpec(memory_space=pltpu.HBM)
    vmem = pl.BlockSpec(memory_space=pltpu.VMEM)
    arrays = (queries, key_rows, value_rows, target)
    arrays += (norm_gain.reshape(HEADS, HEAD_DIM), valid_mask.reshape(1, HEAD_DIM))
    grad_q, grad_k, grad_v, loss = pl.pallas_call(
        kernel,
        out_shape=(whole, whole, whole, jax.ShapeDtypeStruct((8, HEAD_DIM), F32)),
        in_specs=[anywhere] * 6,
        out_specs=(vmem,) * 4,
        scratch_shapes=[full, full, halves, half, half, halves, tile, pltpu.VMEM((1, HEAD_DIM), jnp.int32), tiles(2)]
        + [heads16] * 8
        + [heads] * 5
        + [pltpu.VMEM((4, HEAD_DIM, HEAD_DIM), F32)]
        + [states] * 3
        + [flat] * 4
        + [states] * 2
        + [flat] * 4
        + [tile, tiles(2 * XS), tile, tiles(ZS), tile, tiles(YS)]
        + [
            pltpu.SemaphoreType.DMA((6,)),
            pltpu.SemaphoreType.DMA,
            pltpu.SemaphoreType.DMA((COUNT,)),
            pltpu.SemaphoreType.DMA((COUNT,)),
        ],
        compiler_params=pltpu.CompilerParams(
            collective_id=0, has_side_effects=True, vmem_limit_bytes=VMEM_LIMIT
        ),
        name="linear_attention",
    )(
        *[pltpu.with_memory_space_constraint(array, pltpu.HBM) for array in arrays],
    )
    grad_q, grad_k, grad_v, loss = pl.pallas_call(
        hand_out,
        out_shape=(whole, whole, whole, jax.ShapeDtypeStruct((1, 1), F32)),
        in_specs=[vmem] * 4,
        out_specs=(anywhere,) * 4,
        scratch_shapes=[pltpu.SemaphoreType.DMA((4,)), pltpu.VMEM((1, 1), F32)],
        compiler_params=pltpu.CompilerParams(vmem_limit_bytes=4 * 2**20),
        name="hand_out",
    )(grad_q, grad_k, grad_v, loss)
    return grad_q, grad_k, grad_v, loss.reshape(())


def solution(mesh):
    return jax.shard_map(
        shards,
        mesh=mesh,
        in_specs=(P("seq", "head"),) * 4 + (P("head"), P("seq")),
        out_specs=(P("seq", "head"),) * 3 + (P(),),
        check_vma=False,
    )
```

```python
import jax
import jax.numpy as jnp
from jax import lax
from jax.experimental import pallas as pl
from jax.experimental.pallas import tpu as pltpu
from jax.sharding import PartitionSpec as P

HEAD_DIM = 128
WIDTH = 4096
TOKENS = 8192
HEADS = 8
OWN = 4
CHUNKS = 2
BOTH = OWN // CHUNKS
YS, ZS, XS = 4, 8, 4
CHIPS = YS * ZS
CHUNK_ROWS = BOTH * HEAD_DIM
ROWS = CHUNK_ROWS // CHIPS
EPSILON = 1e-06
VMEM_LIMIT = 24 * 2**20

F32 = jnp.float32
BF16 = jnp.bfloat16
MESH = pl.DeviceIdType.MESH
PAIR, OUT, BACK = 2 * CHUNKS, 0, CHUNKS
FORWARD, REVERSE, INPUTS = 2 * CHUNKS, 0, 5 * CHUNKS
MASK, SUMS, STAT_Z, STAT_Y, RESULTS, COUNT = (INPUTS + n for n in range(1, 7))
LEGS, PAIRED, HALVES, TILES, GRADS, KINDS = range(6)

def ring(delta, count):
    return min(delta, count - delta)


OFFSETS = sorted(
    ((dy, dz) for dy in range(YS) for dz in range(ZS) if dy or dz),
    key=lambda o: -(ring(o[0], YS) + 2 * ring(o[1], ZS)),
)


def split(x):
    high = x.astype(BF16)
    return high, (x - high.astype(F32)).astype(BF16)


def dot3(a, b, contract):
    dims = ((contract[:1], contract[1:]), ((), ()))

    def one(x, y):
        return lax.dot_general(x, y, dims, preferred_element_type=F32)

    return one(a[0], b[0]) + (one(a[0], b[1]) + one(a[1], b[0]))


NN, NT, TN = (1, 0), (1, 1), (0, 0)


def kernel(
    q_hbm, k_hbm, v_hbm, t_hbm, gain_hbm, mask_hbm,
    gq_out, gk_out, gv_out, loss_out,
    whole, near, given, weighted, gain, mask_row, mask,
    qh, ql, kh, kl, vh, vl, sh, sl, att, g, grads, acc,
    kv, kv_far, other, legs, recv, part, recv_b, part_b, qg_one,
    row_out, stat_z_out, stat_y_out, tiles,
    load_sems, store_sem, send_sems, recv_sems,
):
    s, x = lax.axis_index("seq"), lax.axis_index("head")
    y, z, c = s // 16, (s // 2) % ZS, s % 2
    me = y * ZS + z
    far = 1 - c
    comb, pre, comb_b, pre_b = (legs.at[n] for n in range(4))
    gq, gk, gv = (grads.at[n] for n in range(3))
    row_in, stat_z, stat_y = (tiles.at[pl.ds(first, n)] for first, n in ((0, 2 * XS), (2 * XS, ZS), (2 * XS + ZS, YS)))

    def at(ty, tz, tc, tx):
        return (ty * 16 + tz * 2 + tc, tx)

    partner = at(y, z, far, x)
    chips = [((y + dy) % YS, (z + dz) % ZS) for dy, dz in OFFSETS]
    across = [at(y, z, tc, (x + d) % XS) for d in (2, 1, 3) for tc in range(2)] + [partner]
    greeted = [at(ty, tz, c, x) for ty, tz in chips] + across
    def heads_of(core):
        return pl.ds(pl.multiple_of(core * OWN * HEAD_DIM, HEAD_DIM), OWN * HEAD_DIM)

    def head(i):
        return pl.ds(pl.multiple_of(i * HEAD_DIM, HEAD_DIM), HEAD_DIM)

    loads = [
        pltpu.make_async_copy(k_hbm, whole.at[0], load_sems.at[0]),
        pltpu.make_async_copy(v_hbm, whole.at[1], load_sems.at[0]),
        pltpu.make_async_copy(q_hbm.at[:, heads_of(c)], near.at[0], load_sems.at[1]),
        pltpu.make_async_copy(t_hbm.at[:, heads_of(c)], near.at[1], load_sems.at[1]),
        pltpu.make_async_copy(gain_hbm, gain, load_sems.at[2]),
        pltpu.make_async_copy(mask_hbm, mask_row, load_sems.at[3]),
    ]
    for copy in loads:
        copy.start()

    barrier = pltpu.get_barrier_semaphore()
    for device in greeted:
        pl.semaphore_signal(barrier, inc=1, device_id=device, device_id_type=MESH)

    def loaded(ref, sem):
        pltpu.make_async_copy(ref, ref, load_sems.at[sem]).wait()

    def send(src, dst, sem, device, kind):
        pltpu.make_async_remote_copy(
            src_ref=src, dst_ref=dst, send_sem=send_sems.at[kind], recv_sem=recv_sems.at[sem],
            device_id=device, device_id_type=MESH,
        ).start()

    def arrived(ref, sem):
        pltpu.make_async_copy(ref, ref, recv_sems.at[sem]).wait()

    def sent(ref, kind):
        pltpu.make_async_copy(ref, ref, send_sems.at[kind]).wait()

    def piece(chunk, i):
        return pl.ds(pl.multiple_of(chunk * CHUNK_ROWS + i * ROWS, ROWS), ROWS)

    all_but_one = pl.ds(0, (CHIPS - 1) * ROWS)

    def rows_of(i):
        return pl.ds(pl.multiple_of(i * HEAD_DIM, HEAD_DIM), HEAD_DIM)

    def spread(comb, recv, base, chunk):
        for ty, tz in chips:
            send(comb.at[piece(chunk, ty * ZS + tz)], recv.at[piece(chunk, me)], base + OUT + chunk, at(ty, tz, c, x), LEGS)
        recv[piece(chunk, me), :] = comb[piece(chunk, me), :]

    def scan(recv, pre, part, base, chunk, reverse):
        arrived(recv.at[all_but_one], base + OUT + chunk)
        total = jnp.zeros((ROWS, HEAD_DIM), F32)
        for i in reversed(range(CHIPS)) if reverse else range(CHIPS):
            pre[piece(chunk, i), :] = total
            total = total + recv[piece(chunk, i), :]
        for ty, tz in chips:
            send(pre.at[piece(chunk, ty * ZS + tz)], part.at[piece(chunk, me)], base + BACK + chunk, at(ty, tz, c, x), LEGS)
        part[piece(chunk, me), :] = pre[piece(chunk, me), :]

    def scanned(part, base, chunk):
        arrived(part.at[all_but_one], base + BACK + chunk)

    loaded(whole, 0)

    def outer_far(i, carry):
        columns = head(far * OWN + i)
        kv_far[i] = dot3(split(whole[0, :, columns]), split(whole[1, :, columns]), TN)
        return carry

    def outer_own(i, carry):
        columns = head(c * OWN + i)
        key, value = split(whole[0, :, columns]), split(whole[1, :, columns])
        kh[c, i], kl[c, i] = key
        vh[c, i], vl[c, i] = value
        kv[i] = dot3(key, value, TN)
        return carry

    lax.fori_loop(0, OWN, outer_far, 0, unroll=2)
    lax.fori_loop(0, OWN, outer_own, 0, unroll=2)
    pl.semaphore_wait(barrier, len(greeted))
    for chunk in range(CHUNKS):
        half = pl.ds(chunk * BOTH, BOTH)
        send(kv_far.at[half], other.at[half], FORWARD + PAIR + chunk, partner, PAIRED)
    for chunk in range(CHUNKS):
        arrived(other.at[pl.ds(0, BOTH)], FORWARD + PAIR + chunk)
        for i in range(chunk * BOTH, (chunk + 1) * BOTH):
            comb[rows_of(i), :] = kv[i] + other[i]
        spread(comb, recv, FORWARD, chunk)

    for n, hbm in enumerate((q_hbm, k_hbm, v_hbm, t_hbm)):
        send(hbm.at[:, heads_of(far)], given.at[n], INPUTS, partner, HALVES)
    loaded(gain, 2)
    loaded(mask_row, 3)
    mask[c] = jnp.broadcast_to(mask_row[...].astype(F32), (8, HEAD_DIM))
    send(mask.at[c], mask.at[c], MASK, partner, TILES)

    token = lax.broadcasted_iota(jnp.int32, (HEAD_DIM, HEAD_DIM), 0)
    column = lax.broadcasted_iota(jnp.int32, (HEAD_DIM, HEAD_DIM), 1)
    causal = token >= column

    def as_columns(row):
        return jnp.transpose(jnp.broadcast_to(row, (HEAD_DIM, HEAD_DIM)))

    def local(b, i, query, target, mask_columns):
        query = split(query)
        qh[b, i], ql[b, i] = query
        scores = jnp.where(causal, dot3(query, (kh[b, i], kl[b, i]), NT), 0.0)
        scores = split(scores)
        sh[b, i], sl[b, i] = scores
        att[b, i] = dot3(scores, (vh[b, i], vl[b, i]), NN)
        weighted[b, i] = gain[pl.ds(c * OWN + i, 1), :] * (mask_columns * target)

    loaded(near, 1)
    mask_near = as_columns(mask[c, 0:1])

    def local_near(i, carry):
        local(c, i, near[0, :, head(i)], near[1, :, head(i)], mask_near)
        return carry

    lax.fori_loop(0, OWN, local_near, 0)
    arrived(given, INPUTS)
    arrived(mask.at[0], MASK)
    mask_far = as_columns(mask[far, 0:1])

    def kv_zero(i):
        return jnp.where(c == 0, kv[i], other[i])

    def local_far(i, carry):
        kh[far, i], kl[far, i] = split(given[1, :, head(i)])
        vh[far, i], vl[far, i] = split(given[2, :, head(i)])
        local(far, i, given[0, :, head(i)], given[3, :, head(i)], mask_far)
        att[1, i] = att[1, i] + dot3((qh[1, i], ql[1, i]), split(kv_zero(i)), NN)
        return carry

    lax.fori_loop(0, OWN, local_far, 0)
    for chunk in range(CHUNKS):
        scan(recv, pre, part, FORWARD, chunk, False)
    acc[...] = jnp.zeros_like(acc)

    def stacked(high, low, i):
        return [part_of[:, i].reshape(2 * HEAD_DIM, HEAD_DIM) for part_of in (high, low)]

    def attend(i, carry):
        prior = split(part[rows_of(i), :])
        both = dot3(stacked(qh, ql, i), prior, NN)
        for b in range(2):
            row = att[b, i] + both[b * HEAD_DIM : (b + 1) * HEAD_DIM]
            att[b, i] = row
            acc[b] = acc[b] + row * row
            acc[2 + b] = acc[2 + b] + weighted[b, i] * row
        return carry

    for chunk in range(CHUNKS):
        scanned(part, FORWARD, chunk)
        lax.fori_loop(chunk * BOTH, (chunk + 1) * BOTH, attend, 0, unroll=True)
    row_out[...] = jnp.zeros_like(row_out)
    for n in range(4):
        row_out[pl.ds(n, 1), :] = jnp.sum(jnp.transpose(acc[n]), axis=0, keepdims=True)
    for device in across:
        send(row_out, row_in.at[x * 2 + c], SUMS, device, TILES)
    row_in[x * 2 + c] = row_out[...]
    arrived(row_in.at[pl.ds(0, 2 * XS - 1)], SUMS)
    rows = jnp.sum(row_in[...], axis=0)
    inverse = lax.rsqrt(rows[0:2] / WIDTH + EPSILON)
    gain_dots = rows[2:4]
    slope = inverse * inverse * gain_dots / WIDTH
    stat_z_out[...] = jnp.zeros_like(stat_z_out)
    stat_z_out[pl.ds(0, 1), :] = jnp.sum(inverse * gain_dots, axis=0, keepdims=True)
    stat_z_out[pl.ds(1, 1), :] = mask[0, 0:1] + mask[1, 0:1]
    for d in range(1, ZS):
        send(stat_z_out, stat_z.at[z], STAT_Z, at(y, (z + d) % ZS, c, x), TILES)
    stat_z[z] = stat_z_out[...]
    inverse_columns = [as_columns(inverse[b : b + 1]) for b in range(2)]
    slope_columns = [as_columns(slope[b : b + 1]) for b in range(2)]

    def outer_qg(i, carry):
        outer = []
        for b in range(2):
            grad = inverse_columns[b] * (weighted[b, i] - att[b, i] * slope_columns[b])
            g[b, i] = grad
            outer.append(dot3((qh[b, i], ql[b, i]), split(grad), TN))
        qg_one[i] = outer[1]
        comb_b[rows_of(i), :] = outer[0] + outer[1]
        return carry

    for chunk in range(CHUNKS):
        lax.fori_loop(chunk * BOTH, (chunk + 1) * BOTH, outer_qg, 0, unroll=True)
        spread(comb_b, recv_b, REVERSE, chunk)
    def local_grads(i, carry):
        prior = part[rows_of(i), :]
        for b in range(2):
            grad = split(g[b, i])
            query, key, value = (qh[b, i], ql[b, i]), (kh[b, i], kl[b, i]), (vh[b, i], vl[b, i])
            grad_scores = split(jnp.where(causal, dot3(grad, value, NT), 0.0))
            before = split(prior if b == 0 else prior + kv_zero(i))
            gq[b, i] = dot3(grad_scores, key, NN) + dot3(grad, before, NT)
            grad_key = dot3(grad_scores, query, TN)
            grad_value = dot3((sh[b, i], sl[b, i]), grad, TN)
            if b == 0:
                after = split(qg_one[i])
                grad_key = grad_key + dot3(value, after, NT)
                grad_value = grad_value + dot3(key, after, NN)
            gk[b, i] = grad_key
            gv[b, i] = grad_value
        return carry

    lax.fori_loop(0, OWN, local_grads, 0)
    arrived(stat_z.at[pl.ds(0, ZS - 1)], STAT_Z)
    stat_y_out[...] = jnp.sum(stat_z[...], axis=0)
    for d in range(1, YS):
        send(stat_y_out, stat_y.at[y], STAT_Y, at((y + d) % YS, z, c, x), TILES)
    stat_y[y] = stat_y_out[...]
    for chunk in range(CHUNKS):
        scan(recv_b, pre_b, part_b, REVERSE, chunk, True)
    arrived(stat_y.at[pl.ds(0, YS - 1)], STAT_Y)
    totals = jnp.sum(stat_y[...], axis=0)
    token_total = jnp.sum(totals[1:2], axis=1, keepdims=True)
    loss_out[...] = jnp.broadcast_to(jnp.sum(totals[0:1], axis=1, keepdims=True) / token_total, loss_out.shape)
    scale = TOKENS / token_total

    def store(block, out, i):
        columns = head(c * OWN + i)
        send(block.at[far, i], out.at[:, columns], RESULTS, partner, GRADS)
        pltpu.make_async_copy(block.at[c, i], out.at[:, columns], store_sem).start()

    def scaled(i, carry):
        for b in range(2):
            gq[b, i] = gq[b, i] * scale
        store(gq, gq_out, i)
        return carry

    lax.fori_loop(0, OWN, scaled, 0)

    def last(chunk):
        for i in range(chunk * BOTH, (chunk + 1) * BOTH):
            later = split(part_b[rows_of(i), :])
            grad_keys = [gk[b, i] + dot3((vh[b, i], vl[b, i]), later, NT) for b in range(2)]
            grad_values = [gv[b, i] + dot3((kh[b, i], kl[b, i]), later, NN) for b in range(2)]
            for b in range(2):
                gk[b, i] = grad_keys[b] * scale
                gv[b, i] = grad_values[b] * scale
            store(gk, gk_out, i)
            store(gv, gv_out, i)

    for chunk in range(CHUNKS):
        scanned(part_b, REVERSE, chunk)
        last(chunk)
    sent(legs.at[:, pl.ds(0, (CHIPS - 1) * ROWS * CHUNKS)], LEGS)
    sent(kv_far, PAIRED)
    sent(given, HALVES)
    sent(tiles.at[pl.ds(0, 1 + 2 * XS - 1 + ZS - 1 + YS - 1)], TILES)
    half = grads.at[:, 0]
    sent(half, GRADS)
    pltpu.make_async_copy(half, half, store_sem).wait()
    arrived(half, RESULTS)


def hand_out(*refs):
    given, outs, sems, loss = refs[:4], refs[4:8], refs[8], refs[9]
    loss[...] = given[3][0:1, 0:1]
    copies = [pltpu.make_async_copy(loss, outs[3], sems.at[3])]
    copies += [pltpu.make_async_copy(given[n], outs[n], sems.at[n]) for n in range(3)]
    for copy in copies:
        copy.start()
    for copy in copies:
        copy.wait()


def shards(queries, key_rows, value_rows, target, norm_gain, valid_mask):
    whole = jax.ShapeDtypeStruct(queries.shape, F32)
    heads = pltpu.VMEM((2, OWN, HEAD_DIM, HEAD_DIM), F32)
    heads16 = pltpu.VMEM((2, OWN, HEAD_DIM, HEAD_DIM), BF16)
    states = pltpu.VMEM((OWN, HEAD_DIM, HEAD_DIM), F32)
    flat = pltpu.VMEM((OWN * HEAD_DIM, HEAD_DIM), F32)

    def tiles(count):
        return pltpu.VMEM((count, 8, HEAD_DIM), F32)

    def halves(count):
        return pltpu.VMEM((count, HEAD_DIM, OWN * HEAD_DIM), F32)

    tile = pltpu.VMEM((8, HEAD_DIM), F32)
    anywhere = pl.BlockSpec(memory_space=pltpu.HBM)
    vmem = pl.BlockSpec(memory_space=pltpu.VMEM)
    arrays = (queries, key_rows, value_rows, target)
    arrays += (norm_gain.reshape(HEADS, HEAD_DIM), valid_mask.reshape(1, HEAD_DIM))
    grad_q, grad_k, grad_v, loss = pl.pallas_call(
        kernel,
        out_shape=(whole, whole, whole, jax.ShapeDtypeStruct((8, HEAD_DIM), F32)),
        in_specs=[anywhere] * 6,
        out_specs=(vmem,) * 4,
        scratch_shapes=[
            pltpu.VMEM((2, HEAD_DIM, HEADS * HEAD_DIM), F32),
            halves(2), halves(4), heads,
            tile, pltpu.VMEM((1, HEAD_DIM), jnp.int32), tiles(2),
        ]
        + [heads16] * 8
        + [heads] * 2
        + [pltpu.VMEM((3, 2, OWN, HEAD_DIM, HEAD_DIM), F32), pltpu.VMEM((4, HEAD_DIM, HEAD_DIM), F32)]
        + [states] * 3
        + [pltpu.VMEM((4, OWN * HEAD_DIM, HEAD_DIM), F32)]
        + [flat] * 4
        + [states]
        + [tile] * 3
        + [tiles(2 * XS + ZS + YS)]
        + [
            pltpu.SemaphoreType.DMA((4,)),
            pltpu.SemaphoreType.DMA,
            pltpu.SemaphoreType.DMA((KINDS,)),
            pltpu.SemaphoreType.DMA((COUNT,)),
        ],
        compiler_params=pltpu.CompilerParams(
            collective_id=0, has_side_effects=True, vmem_limit_bytes=VMEM_LIMIT
        ),
        name="linear_attention",
    )(
        *[pltpu.with_memory_space_constraint(array, pltpu.HBM) for array in arrays],
    )
    grad_q, grad_k, grad_v, loss = pl.pallas_call(
        hand_out,
        out_shape=(whole, whole, whole, jax.ShapeDtypeStruct((1, 1), F32)),
        in_specs=[vmem] * 4,
        out_specs=(anywhere,) * 4,
        scratch_shapes=[pltpu.SemaphoreType.DMA((4,)), pltpu.VMEM((1, 1), F32)],
        compiler_params=pltpu.CompilerParams(vmem_limit_bytes=4 * 2**20),
        name="hand_out",
    )(grad_q, grad_k, grad_v, loss)
    return grad_q, grad_k, grad_v, loss.reshape(())


def solution(mesh):
    return jax.shard_map(
        shards,
        mesh=mesh,
        in_specs=(P("seq", "head"),) * 4 + (P("head"), P("seq")),
        out_specs=(P("seq", "head"),) * 3 + (P(),),
        check_vma=False,
    )
```

```python
import jax
import jax.numpy as jnp
from jax import lax
from jax.experimental import pallas as pl
from jax.experimental.pallas import tpu as pltpu
from jax.sharding import PartitionSpec as P

HEAD_DIM = 128
WIDTH = 4096
TOKENS = 8192
HEADS = 8
OWN = 4
CHUNKS = 2
BOTH = OWN // CHUNKS
YS, ZS, XS = 4, 8, 4
CHIPS = YS * ZS
CHUNK_ROWS = BOTH * HEAD_DIM
ROWS = CHUNK_ROWS // CHIPS
EPSILON = 1e-06
VMEM_LIMIT = 24 * 2**20

F32 = jnp.float32
BF16 = jnp.bfloat16
MESH = pl.DeviceIdType.MESH
PAIR, OUT, BACK = 2 * CHUNKS, 0, CHUNKS
FORWARD, REVERSE, INPUTS = 2 * CHUNKS, 0, 5 * CHUNKS
MASK, SUMS, STAT_Z, STAT_Y, RESULTS, COUNT = (INPUTS + n for n in range(1, 7))
LEGS, PAIRED, HALVES, TILES, GRADS, KINDS = range(6)

def ring(delta, count):
    return min(delta, count - delta)


OFFSETS = sorted(
    ((dy, dz) for dy in range(YS) for dz in range(ZS) if dy or dz),
    key=lambda o: -(ring(o[0], YS) + 2 * ring(o[1], ZS)),
)


def split(x):
    high = x.astype(BF16)
    return high, (x - high.astype(F32)).astype(BF16)


def dot3(a, b, contract):
    dims = ((contract[:1], contract[1:]), ((), ()))

    def one(x, y):
        return lax.dot_general(x, y, dims, preferred_element_type=F32)

    return one(a[0], b[0]) + (one(a[0], b[1]) + one(a[1], b[0]))


NN, NT, TN = (1, 0), (1, 1), (0, 0)


def kernel(
    q_hbm, k_hbm, v_hbm, t_hbm, gain_hbm, mask_hbm,
    gq_out, gk_out, gv_out, loss_out,
    whole, near, given, weighted, gain, mask_row, mask,
    qh, ql, kh, kl, vh, vl, sh, sl, att, g, grads, acc,
    kv, kv_far, other, legs, recv, part, recv_b, part_b, qg_one,
    leaving, row_out, stat_z_out, stat_y_out, tiles,
    load_sems, store_sem, send_sems, recv_sems,
):
    s, x = lax.axis_index("seq"), lax.axis_index("head")
    y, z, c = s // 16, (s // 2) % ZS, s % 2
    me = y * ZS + z
    far = 1 - c
    comb, pre, comb_b, pre_b = (legs.at[n] for n in range(4))
    gq, gk, gv = (grads.at[n] for n in range(3))
    row_in, stat_z, stat_y = (tiles.at[pl.ds(first, n)] for first, n in ((0, 2 * XS), (2 * XS, ZS), (2 * XS + ZS, YS)))

    def at(ty, tz, tc, tx):
        return (ty * 16 + tz * 2 + tc, tx)

    partner = at(y, z, far, x)
    chips = [((y + dy) % YS, (z + dz) % ZS) for dy, dz in OFFSETS]
    across = [at(y, z, tc, (x + d) % XS) for d in (2, 1, 3) for tc in range(2)] + [partner]
    greeted = [at(ty, tz, c, x) for ty, tz in chips] + across
    def heads_of(core):
        return pl.ds(pl.multiple_of(core * OWN * HEAD_DIM, HEAD_DIM), OWN * HEAD_DIM)

    def head(i):
        return pl.ds(pl.multiple_of(i * HEAD_DIM, HEAD_DIM), HEAD_DIM)

    loads = [
        pltpu.make_async_copy(k_hbm, whole.at[0], load_sems.at[0]),
        pltpu.make_async_copy(v_hbm, whole.at[1], load_sems.at[0]),
        pltpu.make_async_copy(q_hbm.at[:, heads_of(c)], near.at[0], load_sems.at[1]),
        pltpu.make_async_copy(t_hbm.at[:, heads_of(c)], near.at[1], load_sems.at[1]),
        pltpu.make_async_copy(gain_hbm, gain, load_sems.at[2]),
        pltpu.make_async_copy(mask_hbm, mask_row, load_sems.at[3]),
    ]
    for copy in loads:
        copy.start()

    barrier = pltpu.get_barrier_semaphore()
    for device in greeted:
        pl.semaphore_signal(barrier, inc=1, device_id=device, device_id_type=MESH)

    def loaded(ref, sem):
        pltpu.make_async_copy(ref, ref, load_sems.at[sem]).wait()

    def send(src, dst, sem, device, kind):
        pltpu.make_async_remote_copy(
            src_ref=src, dst_ref=dst, send_sem=send_sems.at[kind], recv_sem=recv_sems.at[sem],
            device_id=device, device_id_type=MESH,
        ).start()

    def arrived(ref, sem):
        pltpu.make_async_copy(ref, ref, recv_sems.at[sem]).wait()

    def sent(ref, kind):
        pltpu.make_async_copy(ref, ref, send_sems.at[kind]).wait()

    def piece(chunk, i):
        return pl.ds(pl.multiple_of(chunk * CHUNK_ROWS + i * ROWS, ROWS), ROWS)

    all_but_one = pl.ds(0, (CHIPS - 1) * ROWS)

    def rows_of(i):
        return pl.ds(pl.multiple_of(i * HEAD_DIM, HEAD_DIM), HEAD_DIM)

    def spread(comb, recv, base, chunk):
        for ty, tz in chips:
            send(comb.at[piece(chunk, ty * ZS + tz)], recv.at[piece(chunk, me)], base + OUT + chunk, at(ty, tz, c, x), LEGS)
        recv[piece(chunk, me), :] = comb[piece(chunk, me), :]

    def scan(recv, pre, part, base, chunk, reverse):
        arrived(recv.at[all_but_one], base + OUT + chunk)
        total = jnp.zeros((ROWS, HEAD_DIM), F32)
        for i in reversed(range(CHIPS)) if reverse else range(CHIPS):
            pre[piece(chunk, i), :] = total
            total = total + recv[piece(chunk, i), :]
        for ty, tz in chips:
            send(pre.at[piece(chunk, ty * ZS + tz)], part.at[piece(chunk, me)], base + BACK + chunk, at(ty, tz, c, x), LEGS)
        part[piece(chunk, me), :] = pre[piece(chunk, me), :]

    def scanned(part, base, chunk):
        arrived(part.at[all_but_one], base + BACK + chunk)

    loaded(whole, 0)

    def outer_far(i, carry):
        columns = head(far * OWN + i)
        kv_far[i] = dot3(split(whole[0, :, columns]), split(whole[1, :, columns]), TN)
        return carry

    def outer_own(i, carry):
        columns = head(c * OWN + i)
        key, value = split(whole[0, :, columns]), split(whole[1, :, columns])
        kh[c, i], kl[c, i] = key
        vh[c, i], vl[c, i] = value
        kv[i] = dot3(key, value, TN)
        return carry

    lax.fori_loop(0, OWN, outer_far, 0, unroll=True)
    lax.fori_loop(0, OWN, outer_own, 0, unroll=True)
    pl.semaphore_wait(barrier, len(greeted))
    for chunk in range(CHUNKS):
        half = pl.ds(chunk * BOTH, BOTH)
        send(kv_far.at[half], other.at[half], FORWARD + PAIR + chunk, partner, PAIRED)
    for chunk in range(CHUNKS):
        arrived(other.at[pl.ds(0, BOTH)], FORWARD + PAIR + chunk)
        for i in range(chunk * BOTH, (chunk + 1) * BOTH):
            comb[rows_of(i), :] = kv[i] + other[i]
        spread(comb, recv, FORWARD, chunk)

    for n, hbm in enumerate((q_hbm, k_hbm, v_hbm, t_hbm)):
        send(hbm.at[:, heads_of(far)], given.at[n], INPUTS, partner, HALVES)
    loaded(gain, 2)
    loaded(mask_row, 3)
    mask[c] = jnp.broadcast_to(mask_row[...].astype(F32), (8, HEAD_DIM))
    send(mask.at[c], mask.at[c], MASK, partner, TILES)

    token = lax.broadcasted_iota(jnp.int32, (HEAD_DIM, HEAD_DIM), 0)
    column = lax.broadcasted_iota(jnp.int32, (HEAD_DIM, HEAD_DIM), 1)
    causal = token >= column

    def as_columns(row):
        return jnp.transpose(jnp.broadcast_to(row, (HEAD_DIM, HEAD_DIM)))

    def local(b, i, query, target, mask_columns):
        query = split(query)
        qh[b, i], ql[b, i] = query
        scores = jnp.where(causal, dot3(query, (kh[b, i], kl[b, i]), NT), 0.0)
        scores = split(scores)
        sh[b, i], sl[b, i] = scores
        att[b, i] = dot3(scores, (vh[b, i], vl[b, i]), NN)
        weighted[b, i] = gain[pl.ds(c * OWN + i, 1), :] * (mask_columns * target)

    loaded(near, 1)
    mask_near = as_columns(mask[c, 0:1])

    def local_near(i, carry):
        local(c, i, near[0, :, head(i)], near[1, :, head(i)], mask_near)
        return carry

    lax.fori_loop(0, OWN, local_near, 0, unroll=2)
    arrived(given, INPUTS)
    arrived(mask.at[0], MASK)
    mask_far = as_columns(mask[far, 0:1])

    def kv_zero(i):
        return jnp.where(c == 0, kv[i], other[i])

    def local_far(i, carry):
        kh[far, i], kl[far, i] = split(given[1, :, head(i)])
        vh[far, i], vl[far, i] = split(given[2, :, head(i)])
        local(far, i, given[0, :, head(i)], given[3, :, head(i)], mask_far)
        att[1, i] = att[1, i] + dot3((qh[1, i], ql[1, i]), split(kv_zero(i)), NN)
        return carry

    lax.fori_loop(0, OWN, local_far, 0, unroll=2)
    for chunk in range(CHUNKS):
        scan(recv, pre, part, FORWARD, chunk, False)
    acc[...] = jnp.zeros_like(acc)

    def stacked(high, low, i):
        return [part_of[:, i].reshape(2 * HEAD_DIM, HEAD_DIM) for part_of in (high, low)]

    def attend(i, carry):
        prior = split(part[rows_of(i), :])
        both = dot3(stacked(qh, ql, i), prior, NN)
        for b in range(2):
            row = att[b, i] + both[b * HEAD_DIM : (b + 1) * HEAD_DIM]
            att[b, i] = row
            acc[b] = acc[b] + row * row
            acc[2 + b] = acc[2 + b] + weighted[b, i] * row
        return carry

    for chunk in range(CHUNKS):
        scanned(part, FORWARD, chunk)
        lax.fori_loop(chunk * BOTH, (chunk + 1) * BOTH, attend, 0, unroll=True)
    row_out[...] = jnp.zeros_like(row_out)
    for n in range(4):
        row_out[pl.ds(n, 1), :] = jnp.sum(jnp.transpose(acc[n]), axis=0, keepdims=True)
    for device in across:
        send(row_out, row_in.at[x * 2 + c], SUMS, device, TILES)
    row_in[x * 2 + c] = row_out[...]
    arrived(row_in.at[pl.ds(0, 2 * XS - 1)], SUMS)
    rows = jnp.sum(row_in[...], axis=0)
    inverse = lax.rsqrt(rows[0:2] / WIDTH + EPSILON)
    gain_dots = rows[2:4]
    slope = inverse * inverse * gain_dots / WIDTH
    stat_z_out[...] = jnp.zeros_like(stat_z_out)
    stat_z_out[pl.ds(0, 1), :] = jnp.sum(inverse * gain_dots, axis=0, keepdims=True)
    stat_z_out[pl.ds(1, 1), :] = mask[0, 0:1] + mask[1, 0:1]
    for d in range(1, ZS):
        send(stat_z_out, stat_z.at[z], STAT_Z, at(y, (z + d) % ZS, c, x), TILES)
    stat_z[z] = stat_z_out[...]
    inverse_columns = [as_columns(inverse[b : b + 1]) for b in range(2)]
    slope_columns = [as_columns(slope[b : b + 1]) for b in range(2)]

    def outer_qg(i, carry):
        outer = []
        for b in range(2):
            grad = inverse_columns[b] * (weighted[b, i] - att[b, i] * slope_columns[b])
            g[b, i] = grad
            outer.append(dot3((qh[b, i], ql[b, i]), split(grad), TN))
        qg_one[i] = outer[1]
        comb_b[rows_of(i), :] = outer[0] + outer[1]
        return carry

    for chunk in range(CHUNKS):
        lax.fori_loop(chunk * BOTH, (chunk + 1) * BOTH, outer_qg, 0, unroll=True)
        spread(comb_b, recv_b, REVERSE, chunk)
    def local_grads(i, carry):
        prior = part[rows_of(i), :]
        for b in range(2):
            grad = split(g[b, i])
            query, key, value = (qh[b, i], ql[b, i]), (kh[b, i], kl[b, i]), (vh[b, i], vl[b, i])
            grad_scores = split(jnp.where(causal, dot3(grad, value, NT), 0.0))
            before = split(prior if b == 0 else prior + kv_zero(i))
            gq[b, i] = dot3(grad_scores, key, NN) + dot3(grad, before, NT)
            grad_key = dot3(grad_scores, query, TN)
            grad_value = dot3((sh[b, i], sl[b, i]), grad, TN)
            if b == 0:
                after = split(qg_one[i])
                grad_key = grad_key + dot3(value, after, NT)
                grad_value = grad_value + dot3(key, after, NN)
            gk[b, i] = grad_key
            gv[b, i] = grad_value
        return carry

    lax.fori_loop(0, OWN, local_grads, 0, unroll=2)
    arrived(stat_z.at[pl.ds(0, ZS - 1)], STAT_Z)
    stat_y_out[...] = jnp.sum(stat_z[...], axis=0)
    for d in range(1, YS):
        send(stat_y_out, stat_y.at[y], STAT_Y, at((y + d) % YS, z, c, x), TILES)
    stat_y[y] = stat_y_out[...]
    for chunk in range(CHUNKS):
        scan(recv_b, pre_b, part_b, REVERSE, chunk, True)
    arrived(stat_y.at[pl.ds(0, YS - 1)], STAT_Y)
    totals = jnp.sum(stat_y[...], axis=0)
    token_total = jnp.sum(totals[1:2], axis=1, keepdims=True)
    loss_out[...] = jnp.broadcast_to(jnp.sum(totals[0:1], axis=1, keepdims=True) / token_total, loss_out.shape)
    scale = TOKENS / token_total

    def columns_of(i):
        return head(c * OWN + i)

    def hand_over(block, out, i):
        send(block, out.at[:, columns_of(i)], RESULTS, partner, GRADS)

    def scaled(i, carry):
        for b in range(2):
            gq[b, i] = gq[b, i] * scale
        hand_over(gq.at[far, i], gq_out, i)
        pltpu.make_async_copy(gq.at[c, i], gq_out.at[:, columns_of(i)], store_sem).start()
        return carry

    lax.fori_loop(0, OWN, scaled, 0)

    def last(chunk):
        heads = range(chunk * BOTH, (chunk + 1) * BOTH)
        later = [split(part_b[rows_of(i), :]) for i in heads]

        def finished(b):
            keys = [gk[b, i] + dot3((vh[b, i], vl[b, i]), r, NT) for i, r in zip(heads, later)]
            values = [gv[b, i] + dot3((kh[b, i], kl[b, i]), r, NN) for i, r in zip(heads, later)]
            return keys, values

        for n, done in enumerate(finished(far)):
            for i, grad in zip(heads, done):
                leaving[n, i] = grad * scale
        for n, out in enumerate((gk_out, gv_out)):
            for i in heads:
                hand_over(leaving.at[n, i], out, i)
        for out, done in zip((gk_out, gv_out), finished(c)):
            for i, grad in zip(heads, done):
                out[:, columns_of(i)] = grad * scale

    for chunk in range(CHUNKS):
        scanned(part_b, REVERSE, chunk)
        last(chunk)
    sent(legs.at[:, pl.ds(0, (CHIPS - 1) * ROWS * CHUNKS)], LEGS)
    sent(kv_far, PAIRED)
    sent(given, HALVES)
    sent(tiles.at[pl.ds(0, 1 + 2 * XS - 1 + ZS - 1 + YS - 1)], TILES)
    half = grads.at[:, 0]
    sent(half, GRADS)
    pltpu.make_async_copy(gq.at[0], gq.at[0], store_sem).wait()
    arrived(half, RESULTS)


def hand_out(*refs):
    given, outs, sems, loss = refs[:4], refs[4:8], refs[8], refs[9]
    loss[...] = given[3][0:1, 0:1]
    copies = [pltpu.make_async_copy(loss, outs[3], sems.at[3])]
    copies += [pltpu.make_async_copy(given[n], outs[n], sems.at[n]) for n in range(3)]
    for copy in copies:
        copy.start()
    for copy in copies:
        copy.wait()


def shards(queries, key_rows, value_rows, target, norm_gain, valid_mask):
    whole = jax.ShapeDtypeStruct(queries.shape, F32)
    heads = pltpu.VMEM((2, OWN, HEAD_DIM, HEAD_DIM), F32)
    heads16 = pltpu.VMEM((2, OWN, HEAD_DIM, HEAD_DIM), BF16)
    states = pltpu.VMEM((OWN, HEAD_DIM, HEAD_DIM), F32)
    flat = pltpu.VMEM((OWN * HEAD_DIM, HEAD_DIM), F32)

    def tiles(count):
        return pltpu.VMEM((count, 8, HEAD_DIM), F32)

    def halves(count):
        return pltpu.VMEM((count, HEAD_DIM, OWN * HEAD_DIM), F32)

    tile = pltpu.VMEM((8, HEAD_DIM), F32)
    anywhere = pl.BlockSpec(memory_space=pltpu.HBM)
    vmem = pl.BlockSpec(memory_space=pltpu.VMEM)
    arrays = (queries, key_rows, value_rows, target)
    arrays += (norm_gain.reshape(HEADS, HEAD_DIM), valid_mask.reshape(1, HEAD_DIM))
    grad_q, grad_k, grad_v, loss = pl.pallas_call(
        kernel,
        out_shape=(whole, whole, whole, jax.ShapeDtypeStruct((8, HEAD_DIM), F32)),
        in_specs=[anywhere] * 6,
        out_specs=(vmem,) * 4,
        scratch_shapes=[
            pltpu.VMEM((2, HEAD_DIM, HEADS * HEAD_DIM), F32),
            halves(2), halves(4), heads,
            tile, pltpu.VMEM((1, HEAD_DIM), jnp.int32), tiles(2),
        ]
        + [heads16] * 8
        + [heads] * 2
        + [pltpu.VMEM((3, 2, OWN, HEAD_DIM, HEAD_DIM), F32), pltpu.VMEM((4, HEAD_DIM, HEAD_DIM), F32)]
        + [states] * 3
        + [pltpu.VMEM((4, OWN * HEAD_DIM, HEAD_DIM), F32)]
        + [flat] * 4
        + [states]
        + [heads]
        + [tile] * 3
        + [tiles(2 * XS + ZS + YS)]
        + [
            pltpu.SemaphoreType.DMA((4,)),
            pltpu.SemaphoreType.DMA,
            pltpu.SemaphoreType.DMA((KINDS,)),
            pltpu.SemaphoreType.DMA((COUNT,)),
        ],
        compiler_params=pltpu.CompilerParams(
            collective_id=0, has_side_effects=True, vmem_limit_bytes=VMEM_LIMIT
        ),
        name="linear_attention",
    )(
        *[pltpu.with_memory_space_constraint(array, pltpu.HBM) for array in arrays],
    )
    grad_q, grad_k, grad_v, loss = pl.pallas_call(
        hand_out,
        out_shape=(whole, whole, whole, jax.ShapeDtypeStruct((1, 1), F32)),
        in_specs=[vmem] * 4,
        out_specs=(anywhere,) * 4,
        scratch_shapes=[pltpu.SemaphoreType.DMA((4,)), pltpu.VMEM((1, 1), F32)],
        compiler_params=pltpu.CompilerParams(vmem_limit_bytes=4 * 2**20),
        name="hand_out",
    )(grad_q, grad_k, grad_v, loss)
    return grad_q, grad_k, grad_v, loss.reshape(())


def solution(mesh):
    return jax.shard_map(
        shards,
        mesh=mesh,
        in_specs=(P("seq", "head"),) * 4 + (P("head"), P("seq")),
        out_specs=(P("seq", "head"),) * 3 + (P(),),
        check_vma=False,
    )
```

```python
import jax
import jax.numpy as jnp
from jax import lax
from jax.experimental import pallas as pl
from jax.experimental.pallas import tpu as pltpu
from jax.sharding import PartitionSpec as P

HEAD_DIM = 128
WIDTH = 4096
TOKENS = 8192
HEADS = 8
OWN = 4
CHUNKS = 2
BOTH = OWN // CHUNKS
YS, ZS, XS = 4, 8, 4
CHIPS = YS * ZS
CHUNK_ROWS = BOTH * HEAD_DIM
ROWS = CHUNK_ROWS // CHIPS
EPSILON = 1e-06
VMEM_LIMIT = 24 * 2**20

F32 = jnp.float32
BF16 = jnp.bfloat16
MESH = pl.DeviceIdType.MESH
PAIR, OUT, BACK = 2 * CHUNKS, 0, CHUNKS
FORWARD, REVERSE, INPUTS = 2 * CHUNKS, 0, 5 * CHUNKS
MASK, SUMS, STAT_Z, STAT_Y, RESULTS, COUNT = (INPUTS + n for n in range(1, 7))
LEGS, PAIRED, HALVES, TILES, GRADS, KINDS = range(6)

def ring(delta, count):
    return min(delta, count - delta)


OFFSETS = sorted(
    ((dy, dz) for dy in range(YS) for dz in range(ZS) if dy or dz),
    key=lambda o: -(2 * ring(o[0], YS) + 3 * ring(o[1], ZS)),
)


def split(x):
    high = x.astype(BF16)
    return high, (x - high.astype(F32)).astype(BF16)


def dot3(a, b, contract):
    dims = ((contract[:1], contract[1:]), ((), ()))

    def one(x, y):
        return lax.dot_general(x, y, dims, preferred_element_type=F32)

    return one(a[0], b[0]) + (one(a[0], b[1]) + one(a[1], b[0]))


NN, NT, TN = (1, 0), (1, 1), (0, 0)


def kernel(
    q_hbm, k_hbm, v_hbm, t_hbm, gain_hbm, mask_hbm,
    gq_out, gk_out, gv_out, loss_out,
    whole, near, given, weighted, gain, mask_row, mask,
    qh, ql, kh, kl, vh, vl, sh, sl, att, g, grads, acc,
    kv, kv_far, other, legs, recv, part, recv_b, part_b, qg_one,
    leaving, row_out, stat_z_out, stat_y_out, tiles,
    load_sems, store_sem, send_sems, recv_sems,
):
    s, x = lax.axis_index("seq"), lax.axis_index("head")
    y, z, c = s // 16, (s // 2) % ZS, s % 2
    me = y * ZS + z
    far = 1 - c
    comb, pre, comb_b, pre_b = (legs.at[n] for n in range(4))
    gq, gk, gv = (grads.at[n] for n in range(3))
    row_in, stat_z, stat_y = (tiles.at[pl.ds(first, n)] for first, n in ((0, 2 * XS), (2 * XS, ZS), (2 * XS + ZS, YS)))

    def at(ty, tz, tc, tx):
        return (ty * 16 + tz * 2 + tc, tx)

    partner = at(y, z, far, x)
    chips = [((y + dy) % YS, (z + dz) % ZS) for dy, dz in OFFSETS]
    across = [at(y, z, tc, (x + d) % XS) for d in (2, 1, 3) for tc in (far, c)] + [partner]
    greeted = [at(ty, tz, c, x) for ty, tz in chips] + across
    def heads_of(core):
        return pl.ds(pl.multiple_of(core * OWN * HEAD_DIM, HEAD_DIM), OWN * HEAD_DIM)

    def head(i):
        return pl.ds(pl.multiple_of(i * HEAD_DIM, HEAD_DIM), HEAD_DIM)

    loads = [
        pltpu.make_async_copy(k_hbm, whole.at[0], load_sems.at[0]),
        pltpu.make_async_copy(v_hbm, whole.at[1], load_sems.at[0]),
        pltpu.make_async_copy(q_hbm.at[:, heads_of(c)], near.at[0], load_sems.at[1]),
        pltpu.make_async_copy(t_hbm.at[:, heads_of(c)], near.at[1], load_sems.at[1]),
        pltpu.make_async_copy(gain_hbm, gain, load_sems.at[2]),
        pltpu.make_async_copy(mask_hbm, mask_row, load_sems.at[3]),
    ]
    for copy in loads:
        copy.start()

    barrier = pltpu.get_barrier_semaphore()
    for device in greeted:
        pl.semaphore_signal(barrier, inc=1, device_id=device, device_id_type=MESH)

    def loaded(ref, sem):
        pltpu.make_async_copy(ref, ref, load_sems.at[sem]).wait()

    def send(src, dst, sem, device, kind):
        pltpu.make_async_remote_copy(
            src_ref=src, dst_ref=dst, send_sem=send_sems.at[kind], recv_sem=recv_sems.at[sem],
            device_id=device, device_id_type=MESH,
        ).start()

    def arrived(ref, sem):
        pltpu.make_async_copy(ref, ref, recv_sems.at[sem]).wait()

    def sent(ref, kind):
        pltpu.make_async_copy(ref, ref, send_sems.at[kind]).wait()

    def piece(chunk, i):
        return pl.ds(pl.multiple_of(chunk * CHUNK_ROWS + i * ROWS, ROWS), ROWS)

    all_but_one = pl.ds(0, (CHIPS - 1) * ROWS)

    def rows_of(i):
        return pl.ds(pl.multiple_of(i * HEAD_DIM, HEAD_DIM), HEAD_DIM)

    def spread(comb, recv, base, chunk):
        for ty, tz in chips:
            send(comb.at[piece(chunk, ty * ZS + tz)], recv.at[piece(chunk, me)], base + OUT + chunk, at(ty, tz, c, x), LEGS)
        recv[piece(chunk, me), :] = comb[piece(chunk, me), :]

    def scan(recv, pre, part, base, chunk, reverse):
        arrived(recv.at[all_but_one], base + OUT + chunk)
        total = jnp.zeros((ROWS, HEAD_DIM), F32)
        for i in reversed(range(CHIPS)) if reverse else range(CHIPS):
            pre[piece(chunk, i), :] = total
            total = total + recv[piece(chunk, i), :]
        for ty, tz in chips:
            send(pre.at[piece(chunk, ty * ZS + tz)], part.at[piece(chunk, me)], base + BACK + chunk, at(ty, tz, c, x), LEGS)
        part[piece(chunk, me), :] = pre[piece(chunk, me), :]

    def scanned(part, base, chunk):
        arrived(part.at[all_but_one], base + BACK + chunk)

    loaded(whole, 0)

    def outer_far(i, carry):
        columns = head(far * OWN + i)
        kv_far[i] = dot3(split(whole[0, :, columns]), split(whole[1, :, columns]), TN)
        return carry

    def outer_own(i, carry):
        columns = head(c * OWN + i)
        key, value = split(whole[0, :, columns]), split(whole[1, :, columns])
        kh[c, i], kl[c, i] = key
        vh[c, i], vl[c, i] = value
        kv[i] = dot3(key, value, TN)
        return carry

    lax.fori_loop(0, OWN, outer_far, 0, unroll=True)
    lax.fori_loop(0, OWN, outer_own, 0, unroll=True)
    pl.semaphore_wait(barrier, len(greeted))
    for chunk in range(CHUNKS):
        half = pl.ds(chunk * BOTH, BOTH)
        send(kv_far.at[half], other.at[half], FORWARD + PAIR + chunk, partner, PAIRED)
    for chunk in range(CHUNKS):
        arrived(other.at[pl.ds(0, BOTH)], FORWARD + PAIR + chunk)
        for i in range(chunk * BOTH, (chunk + 1) * BOTH):
            comb[rows_of(i), :] = kv[i] + other[i]
        spread(comb, recv, FORWARD, chunk)

    for n, hbm in enumerate((q_hbm, k_hbm, v_hbm, t_hbm)):
        send(hbm.at[:, heads_of(far)], given.at[n], INPUTS, partner, HALVES)
    loaded(gain, 2)
    loaded(mask_row, 3)
    mask[c] = jnp.broadcast_to(mask_row[...].astype(F32), (8, HEAD_DIM))
    send(mask.at[c], mask.at[c], MASK, partner, TILES)

    token = lax.broadcasted_iota(jnp.int32, (HEAD_DIM, HEAD_DIM), 0)
    column = lax.broadcasted_iota(jnp.int32, (HEAD_DIM, HEAD_DIM), 1)
    causal = token >= column

    def as_columns(row):
        return jnp.transpose(jnp.broadcast_to(row, (HEAD_DIM, HEAD_DIM)))

    def local(b, i, query, target, mask_columns):
        query = split(query)
        qh[b, i], ql[b, i] = query
        scores = jnp.where(causal, dot3(query, (kh[b, i], kl[b, i]), NT), 0.0)
        scores = split(scores)
        sh[b, i], sl[b, i] = scores
        att[b, i] = dot3(scores, (vh[b, i], vl[b, i]), NN)
        weighted[b, i] = gain[pl.ds(c * OWN + i, 1), :] * (mask_columns * target)

    loaded(near, 1)
    mask_near = as_columns(mask[c, 0:1])

    def local_near(i, carry):
        local(c, i, near[0, :, head(i)], near[1, :, head(i)], mask_near)
        return carry

    lax.fori_loop(0, OWN, local_near, 0, unroll=2)
    arrived(given, INPUTS)
    arrived(mask.at[0], MASK)
    mask_far = as_columns(mask[far, 0:1])

    def kv_zero(i):
        return jnp.where(c == 0, kv[i], other[i])

    def local_far(i, carry):
        kh[far, i], kl[far, i] = split(given[1, :, head(i)])
        vh[far, i], vl[far, i] = split(given[2, :, head(i)])
        local(far, i, given[0, :, head(i)], given[3, :, head(i)], mask_far)
        att[1, i] = att[1, i] + dot3((qh[1, i], ql[1, i]), split(kv_zero(i)), NN)
        return carry

    lax.fori_loop(0, OWN, local_far, 0, unroll=2)
    for chunk in range(CHUNKS):
        scan(recv, pre, part, FORWARD, chunk, False)
    acc[...] = jnp.zeros_like(acc)

    def stacked(high, low, i):
        return [part_of[:, i].reshape(2 * HEAD_DIM, HEAD_DIM) for part_of in (high, low)]

    def attend(i, carry):
        prior = split(part[rows_of(i), :])
        both = dot3(stacked(qh, ql, i), prior, NN)
        for b in range(2):
            row = att[b, i] + both[b * HEAD_DIM : (b + 1) * HEAD_DIM]
            att[b, i] = row
            acc[b] = acc[b] + row * row
            acc[2 + b] = acc[2 + b] + weighted[b, i] * row
        return carry

    for chunk in range(CHUNKS):
        scanned(part, FORWARD, chunk)
        lax.fori_loop(chunk * BOTH, (chunk + 1) * BOTH, attend, 0, unroll=True)
    row_out[...] = jnp.zeros_like(row_out)
    for n in range(4):
        row_out[pl.ds(n, 1), :] = jnp.sum(jnp.transpose(acc[n]), axis=0, keepdims=True)
    for device in across:
        send(row_out, row_in.at[x * 2 + c], SUMS, device, TILES)
    row_in[x * 2 + c] = row_out[...]
    arrived(row_in.at[pl.ds(0, 2 * XS - 1)], SUMS)
    rows = jnp.sum(row_in[...], axis=0)
    inverse = lax.rsqrt(rows[0:2] / WIDTH + EPSILON)
    gain_dots = rows[2:4]
    slope = inverse * inverse * gain_dots / WIDTH
    stat_z_out[...] = jnp.zeros_like(stat_z_out)
    stat_z_out[pl.ds(0, 1), :] = jnp.sum(inverse * gain_dots, axis=0, keepdims=True)
    stat_z_out[pl.ds(1, 1), :] = mask[0, 0:1] + mask[1, 0:1]
    for d in range(1, ZS):
        send(stat_z_out, stat_z.at[z], STAT_Z, at(y, (z + d) % ZS, c, x), TILES)
    stat_z[z] = stat_z_out[...]
    inverse_columns = [as_columns(inverse[b : b + 1]) for b in range(2)]
    slope_columns = [as_columns(slope[b : b + 1]) for b in range(2)]

    def outer_qg(i, carry):
        outer = []
        for b in range(2):
            grad = inverse_columns[b] * (weighted[b, i] - att[b, i] * slope_columns[b])
            g[b, i] = grad
            outer.append(dot3((qh[b, i], ql[b, i]), split(grad), TN))
        qg_one[i] = outer[1]
        comb_b[rows_of(i), :] = outer[0] + outer[1]
        return carry

    for chunk in range(CHUNKS):
        lax.fori_loop(chunk * BOTH, (chunk + 1) * BOTH, outer_qg, 0, unroll=True)
        spread(comb_b, recv_b, REVERSE, chunk)
    def local_grads(i, carry):
        prior = part[rows_of(i), :]
        for b in range(2):
            grad = split(g[b, i])
            query, key, value = (qh[b, i], ql[b, i]), (kh[b, i], kl[b, i]), (vh[b, i], vl[b, i])
            grad_scores = split(jnp.where(causal, dot3(grad, value, NT), 0.0))
            before = split(prior if b == 0 else prior + kv_zero(i))
            gq[b, i] = dot3(grad_scores, key, NN) + dot3(grad, before, NT)
            grad_key = dot3(grad_scores, query, TN)
            grad_value = dot3((sh[b, i], sl[b, i]), grad, TN)
            if b == 0:
                after = split(qg_one[i])
                grad_key = grad_key + dot3(value, after, NT)
                grad_value = grad_value + dot3(key, after, NN)
            gk[b, i] = grad_key
            gv[b, i] = grad_value
        return carry

    lax.fori_loop(0, OWN, local_grads, 0, unroll=2)
    arrived(stat_z.at[pl.ds(0, ZS - 1)], STAT_Z)
    stat_y_out[...] = jnp.sum(stat_z[...], axis=0)
    for d in range(1, YS):
        send(stat_y_out, stat_y.at[y], STAT_Y, at((y + d) % YS, z, c, x), TILES)
    stat_y[y] = stat_y_out[...]
    for chunk in range(CHUNKS):
        scan(recv_b, pre_b, part_b, REVERSE, chunk, True)
    arrived(stat_y.at[pl.ds(0, YS - 1)], STAT_Y)
    totals = jnp.sum(stat_y[...], axis=0)
    token_total = jnp.sum(totals[1:2], axis=1, keepdims=True)
    loss_out[...] = jnp.broadcast_to(jnp.sum(totals[0:1], axis=1, keepdims=True) / token_total, loss_out.shape)
    scale = TOKENS / token_total

    def columns_of(i):
        return head(c * OWN + i)

    def hand_over(block, out, i):
        send(block, out.at[:, columns_of(i)], RESULTS, partner, GRADS)

    def scaled(i, carry):
        for b in range(2):
            gq[b, i] = gq[b, i] * scale
        hand_over(gq.at[far, i], gq_out, i)
        pltpu.make_async_copy(gq.at[c, i], gq_out.at[:, columns_of(i)], store_sem).start()
        return carry

    lax.fori_loop(0, OWN, scaled, 0)

    def last(chunk):
        heads = range(chunk * BOTH, (chunk + 1) * BOTH)
        later = [split(part_b[rows_of(i), :]) for i in heads]

        def finished(b):
            keys = [gk[b, i] + dot3((vh[b, i], vl[b, i]), r, NT) for i, r in zip(heads, later)]
            values = [gv[b, i] + dot3((kh[b, i], kl[b, i]), r, NN) for i, r in zip(heads, later)]
            return keys, values

        for n, done in enumerate(finished(far)):
            for i, grad in zip(heads, done):
                leaving[n, i] = grad * scale
        for n, out in enumerate((gk_out, gv_out)):
            for i in heads:
                hand_over(leaving.at[n, i], out, i)
        for out, done in zip((gk_out, gv_out), finished(c)):
            for i, grad in zip(heads, done):
                out[:, columns_of(i)] = grad * scale

    for chunk in range(CHUNKS):
        scanned(part_b, REVERSE, chunk)
        last(chunk)
    sent(legs.at[:, pl.ds(0, (CHIPS - 1) * ROWS * CHUNKS)], LEGS)
    sent(kv_far, PAIRED)
    sent(given, HALVES)
    sent(tiles.at[pl.ds(0, 1 + 2 * XS - 1 + ZS - 1 + YS - 1)], TILES)
    half = grads.at[:, 0]
    sent(half, GRADS)
    pltpu.make_async_copy(gq.at[0], gq.at[0], store_sem).wait()
    arrived(half, RESULTS)


def hand_out(*refs):
    given, outs, sems, loss = refs[:4], refs[4:8], refs[8], refs[9]
    copies = [pltpu.make_async_copy(given[n], outs[n], sems.at[n]) for n in range(3)]
    copies.append(pltpu.make_async_copy(loss, outs[3], sems.at[3]))
    for copy in copies[:3]:
        copy.start()
    loss[...] = given[3][0:1, 0:1]
    copies[3].start()
    for copy in copies:
        copy.wait()


def shards(queries, key_rows, value_rows, target, norm_gain, valid_mask):
    whole = jax.ShapeDtypeStruct(queries.shape, F32)
    heads = pltpu.VMEM((2, OWN, HEAD_DIM, HEAD_DIM), F32)
    heads16 = pltpu.VMEM((2, OWN, HEAD_DIM, HEAD_DIM), BF16)
    states = pltpu.VMEM((OWN, HEAD_DIM, HEAD_DIM), F32)
    flat = pltpu.VMEM((OWN * HEAD_DIM, HEAD_DIM), F32)

    def tiles(count):
        return pltpu.VMEM((count, 8, HEAD_DIM), F32)

    def halves(count):
        return pltpu.VMEM((count, HEAD_DIM, OWN * HEAD_DIM), F32)

    tile = pltpu.VMEM((8, HEAD_DIM), F32)
    anywhere = pl.BlockSpec(memory_space=pltpu.HBM)
    vmem = pl.BlockSpec(memory_space=pltpu.VMEM)
    arrays = (queries, key_rows, value_rows, target)
    arrays += (norm_gain.reshape(HEADS, HEAD_DIM), valid_mask.reshape(1, HEAD_DIM))
    grad_q, grad_k, grad_v, loss = pl.pallas_call(
        kernel,
        out_shape=(whole, whole, whole, jax.ShapeDtypeStruct((8, HEAD_DIM), F32)),
        in_specs=[anywhere] * 6,
        out_specs=(vmem,) * 4,
        scratch_shapes=[
            pltpu.VMEM((2, HEAD_DIM, HEADS * HEAD_DIM), F32),
            halves(2), halves(4), heads,
            tile, pltpu.VMEM((1, HEAD_DIM), jnp.int32), tiles(2),
        ]
        + [heads16] * 8
        + [heads] * 2
        + [pltpu.VMEM((3, 2, OWN, HEAD_DIM, HEAD_DIM), F32), pltpu.VMEM((4, HEAD_DIM, HEAD_DIM), F32)]
        + [states] * 3
        + [pltpu.VMEM((4, OWN * HEAD_DIM, HEAD_DIM), F32)]
        + [flat] * 4
        + [states]
        + [heads]
        + [tile] * 3
        + [tiles(2 * XS + ZS + YS)]
        + [
            pltpu.SemaphoreType.DMA((4,)),
            pltpu.SemaphoreType.DMA,
            pltpu.SemaphoreType.DMA((KINDS,)),
            pltpu.SemaphoreType.DMA((COUNT,)),
        ],
        compiler_params=pltpu.CompilerParams(
            collective_id=0, has_side_effects=True, vmem_limit_bytes=VMEM_LIMIT
        ),
        name="linear_attention",
    )(
        *[pltpu.with_memory_space_constraint(array, pltpu.HBM) for array in arrays],
    )
    grad_q, grad_k, grad_v, loss = pl.pallas_call(
        hand_out,
        out_shape=(whole, whole, whole, jax.ShapeDtypeStruct((1, 1), F32)),
        in_specs=[vmem] * 4,
        out_specs=(anywhere,) * 4,
        scratch_shapes=[pltpu.SemaphoreType.DMA((4,)), pltpu.VMEM((1, 1), F32)],
        compiler_params=pltpu.CompilerParams(vmem_limit_bytes=4 * 2**20),
        name="hand_out",
    )(grad_q, grad_k, grad_v, loss)
    return grad_q, grad_k, grad_v, loss.reshape(())


def solution(mesh):
    return jax.shard_map(
        shards,
        mesh=mesh,
        in_specs=(P("seq", "head"),) * 4 + (P("head"), P("seq")),
        out_specs=(P("seq", "head"),) * 3 + (P(),),
        check_vma=False,
    )
```

```python
import jax
import jax.numpy as jnp
from jax import lax
from jax.experimental import pallas as pl
from jax.experimental.pallas import tpu as pltpu
from jax.sharding import PartitionSpec as P

HEAD_DIM = 128
WIDTH = 4096
TOKENS = 8192
HEADS = 8
OWN = 4
CHUNKS = 2
BOTH = OWN // CHUNKS
YS, ZS, XS = 4, 8, 4
CHIPS = YS * ZS
CHUNK_ROWS = BOTH * HEAD_DIM
ROWS = CHUNK_ROWS // CHIPS
EPSILON = 1e-06
VMEM_LIMIT = 24 * 2**20

F32 = jnp.float32
BF16 = jnp.bfloat16
MESH = pl.DeviceIdType.MESH
PAIR, OUT, BACK = 2 * CHUNKS, 0, CHUNKS
FORWARD, REVERSE, INPUTS = 2 * CHUNKS, 0, 5 * CHUNKS
MASK, SUMS, STAT_Z, STAT_Y, RESULTS, COUNT = (INPUTS + n for n in range(1, 7))
LEGS, PAIRED, HALVES, TILES, GRADS, KINDS = range(6)

def ring(delta, count):
    return min(delta, count - delta)


OFFSETS = sorted(
    ((dy, dz) for dy in range(YS) for dz in range(ZS) if dy or dz),
    key=lambda o: -(2 * ring(o[0], YS) + 3 * ring(o[1], ZS)),
)


def split(x):
    high = x.astype(BF16)
    return high, (x - high.astype(F32)).astype(BF16)


def dot3(a, b, contract):
    dims = ((contract[:1], contract[1:]), ((), ()))

    def one(x, y):
        return lax.dot_general(x, y, dims, preferred_element_type=F32)

    return one(a[0], b[0]) + (one(a[0], b[1]) + one(a[1], b[0]))


NN, NT, TN = (1, 0), (1, 1), (0, 0)


def kernel(
    q_hbm, k_hbm, v_hbm, t_hbm, gain_hbm, mask_hbm,
    gq_out, gk_out, gv_out, loss_out,
    whole, near, given, weighted, gain, mask_row, mask,
    qh, ql, kh, kl, vh, vl, sh, sl, att, g, grads, acc,
    kv, kv_far, other, legs, recv, part, recv_b, part_b, qg_one,
    leaving, row_out, stat_z_out, stat_y_out, tiles,
    load_sems, store_sem, send_sems, recv_sems,
):
    s, x = lax.axis_index("seq"), lax.axis_index("head")
    y, z, c = s // 16, (s // 2) % ZS, s % 2
    me = y * ZS + z
    far = 1 - c
    comb, pre, comb_b, pre_b = (legs.at[n] for n in range(4))
    gq, gk, gv = (grads.at[n] for n in range(3))
    row_in, stat_z, stat_y = (tiles.at[pl.ds(first, n)] for first, n in ((0, 2 * XS), (2 * XS, ZS), (2 * XS + ZS, YS)))

    def at(ty, tz, tc, tx):
        return (ty * 16 + tz * 2 + tc, tx)

    partner = at(y, z, far, x)
    chips = [((y + dy) % YS, (z + dz) % ZS) for dy, dz in OFFSETS]
    across = [at(y, z, tc, (x + d) % XS) for d in (1, 3, 2) for tc in (far, c)] + [partner]
    greeted = [at(ty, tz, c, x) for ty, tz in chips] + across
    def heads_of(core):
        return pl.ds(pl.multiple_of(core * OWN * HEAD_DIM, HEAD_DIM), OWN * HEAD_DIM)

    def head(i):
        return pl.ds(pl.multiple_of(i * HEAD_DIM, HEAD_DIM), HEAD_DIM)

    loads = [
        pltpu.make_async_copy(k_hbm, whole.at[0], load_sems.at[0]),
        pltpu.make_async_copy(v_hbm, whole.at[1], load_sems.at[0]),
        pltpu.make_async_copy(q_hbm.at[:, heads_of(c)], near.at[0], load_sems.at[1]),
        pltpu.make_async_copy(t_hbm.at[:, heads_of(c)], near.at[1], load_sems.at[1]),
        pltpu.make_async_copy(gain_hbm, gain, load_sems.at[2]),
        pltpu.make_async_copy(mask_hbm, mask_row, load_sems.at[3]),
    ]
    for copy in loads:
        copy.start()

    barrier = pltpu.get_barrier_semaphore()
    for device in greeted:
        pl.semaphore_signal(barrier, inc=1, device_id=device, device_id_type=MESH)

    def loaded(ref, sem):
        pltpu.make_async_copy(ref, ref, load_sems.at[sem]).wait()

    def send(src, dst, sem, device, kind):
        pltpu.make_async_remote_copy(
            src_ref=src, dst_ref=dst, send_sem=send_sems.at[kind], recv_sem=recv_sems.at[sem],
            device_id=device, device_id_type=MESH,
        ).start()

    def arrived(ref, sem):
        pltpu.make_async_copy(ref, ref, recv_sems.at[sem]).wait()

    def sent(ref, kind):
        pltpu.make_async_copy(ref, ref, send_sems.at[kind]).wait()

    def piece(chunk, i):
        return pl.ds(pl.multiple_of(chunk * CHUNK_ROWS + i * ROWS, ROWS), ROWS)

    all_but_one = pl.ds(0, (CHIPS - 1) * ROWS)

    def rows_of(i):
        return pl.ds(pl.multiple_of(i * HEAD_DIM, HEAD_DIM), HEAD_DIM)

    def spread(comb, recv, base, chunk):
        for ty, tz in chips:
            send(comb.at[piece(chunk, ty * ZS + tz)], recv.at[piece(chunk, me)], base + OUT + chunk, at(ty, tz, c, x), LEGS)
        recv[piece(chunk, me), :] = comb[piece(chunk, me), :]

    def scan(recv, pre, part, base, chunk, reverse):
        arrived(recv.at[all_but_one], base + OUT + chunk)
        total = jnp.zeros((ROWS, HEAD_DIM), F32)
        for i in reversed(range(CHIPS)) if reverse else range(CHIPS):
            pre[piece(chunk, i), :] = total
            total = total + recv[piece(chunk, i), :]
        for ty, tz in chips:
            send(pre.at[piece(chunk, ty * ZS + tz)], part.at[piece(chunk, me)], base + BACK + chunk, at(ty, tz, c, x), LEGS)
        part[piece(chunk, me), :] = pre[piece(chunk, me), :]

    def scanned(part, base, chunk):
        arrived(part.at[all_but_one], base + BACK + chunk)

    loaded(whole, 0)

    def outer_far(i, carry):
        columns = head(far * OWN + i)
        kv_far[i] = dot3(split(whole[0, :, columns]), split(whole[1, :, columns]), TN)
        return carry

    def outer_own(i, carry):
        columns = head(c * OWN + i)
        key, value = split(whole[0, :, columns]), split(whole[1, :, columns])
        kh[c, i], kl[c, i] = key
        vh[c, i], vl[c, i] = value
        kv[i] = dot3(key, value, TN)
        return carry

    lax.fori_loop(0, OWN, outer_far, 0, unroll=True)
    lax.fori_loop(0, OWN, outer_own, 0, unroll=True)
    pl.semaphore_wait(barrier, len(greeted))
    for chunk in range(CHUNKS):
        half = pl.ds(chunk * BOTH, BOTH)
        send(kv_far.at[half], other.at[half], FORWARD + PAIR + chunk, partner, PAIRED)
    for chunk in range(CHUNKS):
        arrived(other.at[pl.ds(0, BOTH)], FORWARD + PAIR + chunk)
        for i in range(chunk * BOTH, (chunk + 1) * BOTH):
            comb[rows_of(i), :] = kv[i] + other[i]
        spread(comb, recv, FORWARD, chunk)

    for n, hbm in enumerate((q_hbm, k_hbm, v_hbm, t_hbm)):
        send(hbm.at[:, heads_of(far)], given.at[n], INPUTS, partner, HALVES)
    loaded(gain, 2)
    loaded(mask_row, 3)
    mask[c] = jnp.broadcast_to(mask_row[...].astype(F32), (8, HEAD_DIM))
    send(mask.at[c], mask.at[c], MASK, partner, TILES)

    token = lax.broadcasted_iota(jnp.int32, (HEAD_DIM, HEAD_DIM), 0)
    column = lax.broadcasted_iota(jnp.int32, (HEAD_DIM, HEAD_DIM), 1)
    causal = token >= column

    def as_columns(row):
        return jnp.transpose(jnp.broadcast_to(row, (HEAD_DIM, HEAD_DIM)))

    def local(b, i, query, target, mask_columns):
        query = split(query)
        qh[b, i], ql[b, i] = query
        scores = jnp.where(causal, dot3(query, (kh[b, i], kl[b, i]), NT), 0.0)
        scores = split(scores)
        sh[b, i], sl[b, i] = scores
        att[b, i] = dot3(scores, (vh[b, i], vl[b, i]), NN)
        weighted[b, i] = gain[pl.ds(c * OWN + i, 1), :] * (mask_columns * target)

    loaded(near, 1)
    mask_near = as_columns(mask[c, 0:1])

    def local_near(i, carry):
        local(c, i, near[0, :, head(i)], near[1, :, head(i)], mask_near)
        return carry

    lax.fori_loop(0, OWN, local_near, 0, unroll=2)
    arrived(given, INPUTS)
    arrived(mask.at[0], MASK)
    mask_far = as_columns(mask[far, 0:1])

    def kv_zero(i):
        return jnp.where(c == 0, kv[i], other[i])

    def local_far(i, carry):
        kh[far, i], kl[far, i] = split(given[1, :, head(i)])
        vh[far, i], vl[far, i] = split(given[2, :, head(i)])
        local(far, i, given[0, :, head(i)], given[3, :, head(i)], mask_far)
        att[1, i] = att[1, i] + dot3((qh[1, i], ql[1, i]), split(kv_zero(i)), NN)
        return carry

    lax.fori_loop(0, OWN, local_far, 0, unroll=2)
    for chunk in range(CHUNKS):
        scan(recv, pre, part, FORWARD, chunk, False)
    acc[...] = jnp.zeros_like(acc)

    def stacked(high, low, i):
        return [part_of[:, i].reshape(2 * HEAD_DIM, HEAD_DIM) for part_of in (high, low)]

    def attend(i, carry):
        prior = split(part[rows_of(i), :])
        both = dot3(stacked(qh, ql, i), prior, NN)
        for b in range(2):
            row = att[b, i] + both[b * HEAD_DIM : (b + 1) * HEAD_DIM]
            att[b, i] = row
            acc[b] = acc[b] + row * row
            acc[2 + b] = acc[2 + b] + weighted[b, i] * row
        return carry

    for chunk in range(CHUNKS):
        scanned(part, FORWARD, chunk)
        lax.fori_loop(chunk * BOTH, (chunk + 1) * BOTH, attend, 0, unroll=True)
    row_out[...] = jnp.zeros_like(row_out)
    for n in range(4):
        row_out[pl.ds(n, 1), :] = jnp.sum(jnp.transpose(acc[n]), axis=0, keepdims=True)
    for device in across:
        send(row_out, row_in.at[x * 2 + c], SUMS, device, TILES)
    row_in[x * 2 + c] = row_out[...]
    arrived(row_in.at[pl.ds(0, 2 * XS - 1)], SUMS)
    rows = jnp.sum(row_in[...], axis=0)
    inverse = lax.rsqrt(rows[0:2] / WIDTH + EPSILON)
    gain_dots = rows[2:4]
    slope = inverse * inverse * gain_dots / WIDTH
    stat_z_out[...] = jnp.zeros_like(stat_z_out)
    stat_z_out[pl.ds(0, 1), :] = jnp.sum(inverse * gain_dots, axis=0, keepdims=True)
    stat_z_out[pl.ds(1, 1), :] = mask[0, 0:1] + mask[1, 0:1]
    for d in range(1, ZS):
        send(stat_z_out, stat_z.at[z], STAT_Z, at(y, (z + d) % ZS, c, x), TILES)
    stat_z[z] = stat_z_out[...]
    inverse_columns = [as_columns(inverse[b : b + 1]) for b in range(2)]
    slope_columns = [as_columns(slope[b : b + 1]) for b in range(2)]

    def outer_qg(i, carry):
        outer = []
        for b in range(2):
            grad = inverse_columns[b] * (weighted[b, i] - att[b, i] * slope_columns[b])
            g[b, i] = grad
            outer.append(dot3((qh[b, i], ql[b, i]), split(grad), TN))
        qg_one[i] = outer[1]
        comb_b[rows_of(i), :] = outer[0] + outer[1]
        return carry

    for chunk in range(CHUNKS):
        lax.fori_loop(chunk * BOTH, (chunk + 1) * BOTH, outer_qg, 0, unroll=True)
        spread(comb_b, recv_b, REVERSE, chunk)
    def local_grads(i, carry):
        prior = part[rows_of(i), :]
        for b in range(2):
            grad = split(g[b, i])
            query, key, value = (qh[b, i], ql[b, i]), (kh[b, i], kl[b, i]), (vh[b, i], vl[b, i])
            grad_scores = split(jnp.where(causal, dot3(grad, value, NT), 0.0))
            before = split(prior if b == 0 else prior + kv_zero(i))
            gq[b, i] = dot3(grad_scores, key, NN) + dot3(grad, before, NT)
            grad_key = dot3(grad_scores, query, TN)
            grad_value = dot3((sh[b, i], sl[b, i]), grad, TN)
            if b == 0:
                after = split(qg_one[i])
                grad_key = grad_key + dot3(value, after, NT)
                grad_value = grad_value + dot3(key, after, NN)
            gk[b, i] = grad_key
            gv[b, i] = grad_value
        return carry

    lax.fori_loop(0, OWN, local_grads, 0, unroll=2)
    arrived(stat_z.at[pl.ds(0, ZS - 1)], STAT_Z)
    stat_y_out[...] = jnp.sum(stat_z[...], axis=0)
    for d in range(1, YS):
        send(stat_y_out, stat_y.at[y], STAT_Y, at((y + d) % YS, z, c, x), TILES)
    stat_y[y] = stat_y_out[...]
    for chunk in range(CHUNKS):
        scan(recv_b, pre_b, part_b, REVERSE, chunk, True)
    arrived(stat_y.at[pl.ds(0, YS - 1)], STAT_Y)
    totals = jnp.sum(stat_y[...], axis=0)
    token_total = jnp.sum(totals[1:2], axis=1, keepdims=True)
    loss_out[...] = jnp.broadcast_to(jnp.sum(totals[0:1], axis=1, keepdims=True) / token_total, loss_out.shape)
    scale = TOKENS / token_total

    def columns_of(i):
        return head(c * OWN + i)

    def hand_over(block, out, i):
        send(block, out.at[:, columns_of(i)], RESULTS, partner, GRADS)

    def scaled(i, carry):
        for b in range(2):
            gq[b, i] = gq[b, i] * scale
        hand_over(gq.at[far, i], gq_out, i)
        pltpu.make_async_copy(gq.at[c, i], gq_out.at[:, columns_of(i)], store_sem).start()
        return carry

    lax.fori_loop(0, OWN, scaled, 0)

    def last(chunk):
        heads = range(chunk * BOTH, (chunk + 1) * BOTH)
        later = [split(part_b[rows_of(i), :]) for i in heads]

        def finished(b):
            keys = [gk[b, i] + dot3((vh[b, i], vl[b, i]), r, NT) for i, r in zip(heads, later)]
            values = [gv[b, i] + dot3((kh[b, i], kl[b, i]), r, NN) for i, r in zip(heads, later)]
            return keys, values

        for n, done in enumerate(finished(far)):
            for i, grad in zip(heads, done):
                leaving[n, i] = grad * scale
        for n, out in enumerate((gk_out, gv_out)):
            for i in heads:
                hand_over(leaving.at[n, i], out, i)
        for out, done in zip((gk_out, gv_out), finished(c)):
            for i, grad in zip(heads, done):
                out[:, columns_of(i)] = grad * scale

    for chunk in range(CHUNKS):
        scanned(part_b, REVERSE, chunk)
        last(chunk)
    sent(legs.at[:, pl.ds(0, (CHIPS - 1) * ROWS * CHUNKS)], LEGS)
    sent(kv_far, PAIRED)
    sent(given, HALVES)
    sent(tiles.at[pl.ds(0, 1 + 2 * XS - 1 + ZS - 1 + YS - 1)], TILES)
    half = grads.at[:, 0]
    sent(half, GRADS)
    pltpu.make_async_copy(gq.at[0], gq.at[0], store_sem).wait()
    arrived(half, RESULTS)


def hand_out(*refs):
    given, outs, sems, loss = refs[:4], refs[4:8], refs[8], refs[9]
    copies = [pltpu.make_async_copy(given[n], outs[n], sems.at[n]) for n in range(3)]
    copies.append(pltpu.make_async_copy(loss, outs[3], sems.at[3]))
    for copy in copies[:3]:
        copy.start()
    loss[...] = given[3][0:1, 0:1]
    copies[3].start()
    for copy in copies:
        copy.wait()


def shards(queries, key_rows, value_rows, target, norm_gain, valid_mask):
    whole = jax.ShapeDtypeStruct(queries.shape, F32)
    heads = pltpu.VMEM((2, OWN, HEAD_DIM, HEAD_DIM), F32)
    heads16 = pltpu.VMEM((2, OWN, HEAD_DIM, HEAD_DIM), BF16)
    states = pltpu.VMEM((OWN, HEAD_DIM, HEAD_DIM), F32)
    flat = pltpu.VMEM((OWN * HEAD_DIM, HEAD_DIM), F32)

    def tiles(count):
        return pltpu.VMEM((count, 8, HEAD_DIM), F32)

    def halves(count):
        return pltpu.VMEM((count, HEAD_DIM, OWN * HEAD_DIM), F32)

    tile = pltpu.VMEM((8, HEAD_DIM), F32)
    anywhere = pl.BlockSpec(memory_space=pltpu.HBM)
    vmem = pl.BlockSpec(memory_space=pltpu.VMEM)
    arrays = (queries, key_rows, value_rows, target)
    arrays += (norm_gain.reshape(HEADS, HEAD_DIM), valid_mask.reshape(1, HEAD_DIM))
    grad_q, grad_k, grad_v, loss = pl.pallas_call(
        kernel,
        out_shape=(whole, whole, whole, jax.ShapeDtypeStruct((8, HEAD_DIM), F32)),
        in_specs=[anywhere] * 6,
        out_specs=(vmem,) * 4,
        scratch_shapes=[
            pltpu.VMEM((2, HEAD_DIM, HEADS * HEAD_DIM), F32),
            halves(2), halves(4), heads,
            tile, pltpu.VMEM((1, HEAD_DIM), jnp.int32), tiles(2),
        ]
        + [heads16] * 8
        + [heads] * 2
        + [pltpu.VMEM((3, 2, OWN, HEAD_DIM, HEAD_DIM), F32), pltpu.VMEM((4, HEAD_DIM, HEAD_DIM), F32)]
        + [states] * 3
        + [pltpu.VMEM((4, OWN * HEAD_DIM, HEAD_DIM), F32)]
        + [flat] * 4
        + [states]
        + [heads]
        + [tile] * 3
        + [tiles(2 * XS + ZS + YS)]
        + [
            pltpu.SemaphoreType.DMA((4,)),
            pltpu.SemaphoreType.DMA,
            pltpu.SemaphoreType.DMA((KINDS,)),
            pltpu.SemaphoreType.DMA((COUNT,)),
        ],
        compiler_params=pltpu.CompilerParams(
            collective_id=0, has_side_effects=True, vmem_limit_bytes=VMEM_LIMIT
        ),
        name="linear_attention",
    )(
        *[pltpu.with_memory_space_constraint(array, pltpu.HBM) for array in arrays],
    )
    grad_q, grad_k, grad_v, loss = pl.pallas_call(
        hand_out,
        out_shape=(whole, whole, whole, jax.ShapeDtypeStruct((1, 1), F32)),
        in_specs=[vmem] * 4,
        out_specs=(anywhere,) * 4,
        scratch_shapes=[pltpu.SemaphoreType.DMA((4,)), pltpu.VMEM((1, 1), F32)],
        compiler_params=pltpu.CompilerParams(vmem_limit_bytes=4 * 2**20),
        name="hand_out",
    )(grad_q, grad_k, grad_v, loss)
    return grad_q, grad_k, grad_v, loss.reshape(())


def solution(mesh):
    return jax.shard_map(
        shards,
        mesh=mesh,
        in_specs=(P("seq", "head"),) * 4 + (P("head"), P("seq")),
        out_specs=(P("seq", "head"),) * 3 + (P(),),
        check_vma=False,
    )
```
